32 devices in a mesh: col: 4 (over z), row: 8 (over y, x, core).
Axes of the slice: x: 2, y: 2, z: 4, core: 2. Of those that a mesh axis runs over, the one named last changes fastest.
Arguments:
- matrix: bfloat16 [24576, 24576], P('row', 'col'), may hold values from -9 to 9
- left_basis: float32 [320, 24576], P(None, ('row', 'col')), may hold values from -6 to 6
- right_basis: float32 [320, 24576], P(None, ('col', 'row')), may hold values from -6 to 6
- right_block: float32 [64, 24576], P(None, ('col', 'row')), may hold values from -6 to 6
Outputs:
- left_blocks: float32 [64, 24576], P(None, ('row', 'col'))
- right_blocks: float32 [64, 24576], P(None, ('col', 'row'))
- factors: float32 [2, 64, 64], replicated
The draws below stay inside these ranges and needn't reach their ends.
All inputs are finite; a program needn't handle non-finite values.
Results may differ from the reference program's by a relative error of at most 0.0041.
Values may be sent and summed in bfloat16 or wider, within the bound.
No kernel may reach another device: no remote copies, remote signals or barrier semaphores. Data moves between devices by JAX's collectives and lax.ppermute only.
A program may use at most 128 MiB of HBM per device.

```python
import math
import jax
import jax.numpy as jnp
from jax import lax

N = 24576
BLOCK = 64
PRIOR = 5
STEPS = 1


def draw_matrix(key, part):
    first_key, second_key, third_key = jax.random.split(jax.random.fold_in(key, 17), 3)
    entries = jnp.clip(jax.random.normal(first_key, (N, N), jnp.float32), -6.0, 6.0)
    spread = math.log(4.0)
    ramp = 1.0 + 2.0 * jnp.arange(N, dtype=jnp.float32) / N
    row_scale = jnp.exp(jax.random.uniform(second_key, (N,), jnp.float32) * spread) * ramp
    col_scale = jnp.exp(jax.random.uniform(third_key, (N,), jnp.float32) * spread) * ramp
    scaled = entries * row_scale[:, None] * col_scale[None, :] / math.sqrt(N)
    scaled = jnp.clip(scaled, -9.0, 9.0)
    return scaled.astype(jnp.bfloat16)


def block_scale(own_key, extent, shards, smallest, largest):
    def one(dim, blocks):
        draws = jax.random.uniform(jax.random.fold_in(jax.random.fold_in(own_key, 6), dim), (blocks,), jnp.float32, smallest / len(shards), largest / len(shards))
        return jnp.repeat(jnp.exp(draws), extent[dim] // blocks).reshape((-1,) + (1,) * (len(extent) - dim - 1))

    level = one(*shards[0])
    for cut in shards[1:]:
        level = level * one(*cut)
    return level


def gaussian(own_key, extent, scale, most, shards=(), held_as=jnp.bfloat16):
    gain = block_scale(own_key, extent, shards, -0.22, 0.18) if shards else 1.0
    array = jax.random.normal(own_key, extent, jnp.float32) * scale * gain
    return jnp.minimum(jnp.maximum(array, -most), most).astype(held_as)


def setup_inputs(seed: int = 0) -> dict:
    arg_keys = jax.random.split(jax.random.key(seed), 5)
    return {
        "matrix": draw_matrix(jax.random.fold_in(arg_keys[4], 71), 0),
        "left_basis": gaussian(arg_keys[1], (PRIOR * BLOCK, N), 1.0, 6.0, ((1, 32),), jnp.float32),
        "right_basis": gaussian(arg_keys[2], (PRIOR * BLOCK, N), 1.0, 6.0, ((1, 32),), jnp.float32),
        "right_block": gaussian(arg_keys[3], (BLOCK, N), 1.0, 6.0, ((1, 32),), jnp.float32),
    }


highest_precision = lax.Precision.HIGHEST

def contract(first, second, contracted):
    return lax.dot_general(first, second, (contracted, ((), ())), precision=highest_precision)

def orthonormalize(image, basis_set):
    coefficients = contract(basis_set, image, ((1,), (1,))) / N
    projected = image - contract(coefficients, basis_set, ((0,), (0,)))
    gram_matrix = contract(projected, projected, ((1,), (1,))) / N
    factor_low = jnp.linalg.cholesky(gram_matrix)
    new_block = lax.linalg.triangular_solve(factor_low, projected, left_side=True, lower=True)
    return (new_block, factor_low)

def reference(matrix, left_basis, right_basis, right_block):
    left_set = left_basis
    right_set = jnp.concatenate([right_basis, right_block], 0)
    current = right_block
    left_found = []
    right_found = []
    factor_list = []
    for iteration in range(STEPS):
        image = lax.dot_general(current.astype(jnp.bfloat16).astype(jnp.float32), matrix.astype(jnp.float32), (((1,), (1,)), ((), ())), preferred_element_type=jnp.float32)
        left_new, left_low = orthonormalize(image, left_set)
        left_set = jnp.concatenate([left_set, left_new], 0)
        coimage = jnp.dot(left_new.astype(jnp.bfloat16).astype(jnp.float32), matrix.astype(jnp.float32), preferred_element_type=jnp.float32)
        right_new, right_low = orthonormalize(coimage, right_set)
        right_set = jnp.concatenate([right_set, right_new], 0)
        current = right_new
        left_found.append(left_new)
        right_found.append(right_new)
        factor_list.append(left_low)
        factor_list.append(right_low)
    return (jnp.concatenate(left_found, 0), jnp.concatenate(right_found, 0), jnp.stack(factor_list))
```

```python
import functools

import jax
import jax.numpy as jnp
from jax import lax
from jax.experimental import pallas as pl
from jax.experimental.pallas import tpu as pltpu
from jax.sharding import PartitionSpec as P

f32 = jnp.float32
bf16 = jnp.bfloat16
CROSS = bf16
ANY = pl.BlockSpec(memory_space=pltpu.HBM)
VMEM = pl.BlockSpec(memory_space=pltpu.VMEM)


def dot16(first, second, dims):
    return lax.dot_general(first, second, (dims, ((), ())), preferred_element_type=f32)


def dot32(first, second, dims):
    return lax.dot_general(first, second, (dims, ((), ())), precision=lax.Precision.HIGHEST, preferred_element_type=f32)


def split(values):
    high = values.astype(bf16)
    return high, (values - high.astype(f32)).astype(bf16)


def limit(mebibytes):
    return pltpu.CompilerParams(vmem_limit_bytes=mebibytes << 20)


def shape(dims, dtype=f32):
    return jax.ShapeDtypeStruct(dims, dtype)


def padded(count):
    return -(-count // 128) * 128


def call(kernel, inputs, outputs, name, specs=None, scratch=(), mebibytes=8):
    return pl.pallas_call(
        kernel,
        in_specs=specs or [VMEM] * len(inputs),
        out_specs=[VMEM] * len(outputs),
        out_shape=outputs,
        scratch_shapes=list(scratch),
        compiler_params=limit(mebibytes),
        name=name,
    )(*inputs)


def swap(values, axis, size, bit):
    return lax.ppermute(values, axis, [(i, i ^ bit) for i in range(size)])


def exchange_sum(values, axis, size, bit):
    while bit < size:
        if bit * 2 < size:
            one, two, three = (swap(values, axis, size, m) for m in (bit, bit * 2, bit * 3))
            values = (values + one) + (two + three)
            bit *= 4
        else:
            values = values + swap(values, axis, size, bit)
            bit *= 2
    return values


HALVES = 2


def fetch_copies(a_hbm, targets, sems, chunks, chunk):
    me = lax.axis_index("col")
    part = chunk // HALVES
    copies = []
    for n, j in enumerate(chunks):
        for h in range(HALVES):
            start = pl.multiple_of((me ^ j) * chunk + h * part, part)
            copies.append(
                pltpu.make_async_copy(
                    a_hbm.at[pl.ds(start, part), :], targets[n].at[pl.ds(h * part, part), :], sems.at[n, h]
                )
            )
    return copies


def fetch(matrix, chunk, j, bases):
    cols = matrix.shape[1]
    flat = [b for group in bases for b in group]
    width = flat[0].shape[1]
    counts = [sum(b.shape[0] for b in group) for group in bases]
    n_flat = len(flat)

    def kernel(a_hbm, *rest):
        sources, target, outs = rest[:n_flat], rest[n_flat], rest[n_flat + 1 : -n_flat - 2]
        held, sems, base_sems = rest[-n_flat - 2 : -2], rest[-2], rest[-1]
        brought = [pltpu.make_async_copy(src, dst, base_sems.at[n]) for n, (src, dst) in enumerate(zip(sources, held))]
        copies = fetch_copies(a_hbm, [target], sems, [j], chunk)
        for copy in brought + copies:
            copy.start()
        n_base = 0
        for n, group in enumerate(bases):
            rows_high, rows_low, turned = outs[3 * n : 3 * n + 3]
            size = padded(counts[n])
            if counts[n] != size:
                rows_high[...] = jnp.zeros_like(rows_high)
                rows_low[...] = jnp.zeros_like(rows_low)
                turned[...] = jnp.zeros_like(turned)
            at = 0
            for _ in group:
                brought[n_base].wait()
                values = held[n_base][...]
                n_base += 1
                count = values.shape[0]
                high, low = split(values)
                rows_high[at : at + count, :] = high
                rows_low[at : at + count, :] = low
                high, low = split(values.T)
                turned[:, at : at + count] = high
                turned[:, size + at : size + at + count] = low
                at += count
        for copy in copies:
            copy.wait()

    outputs = [shape((chunk, cols), bf16)]
    for count in counts:
        size = padded(count)
        outputs += [shape((size, width), bf16), shape((size, width), bf16), shape((width, 2 * size), bf16)]
    return call(
        kernel,
        [matrix] + flat,
        outputs,
        "fetch",
        specs=[ANY] * (1 + n_flat),
        scratch=[pltpu.VMEM(b.shape, f32) for b in flat]
        + [pltpu.SemaphoreType.DMA((1, HALVES)), pltpu.SemaphoreType.DMA((n_flat,))],
    )


def forward(lefts, order, held, matrix, chunk, products, brought):
    cols = matrix.shape[1]
    block = lefts[0].shape[0]
    step = chunk // 3 if chunk % 384 == 0 else chunk

    def kernel(*rest):
        rest = list(rest)
        parts = [rest.pop(0) for _ in lefts]
        chunks = {j: rest.pop(0) for j in held}
        a_hbm = rest.pop(0)
        outs = [rest.pop(0) for _ in products]
        targets = [rest.pop(0) for _ in brought]
        copies = fetch_copies(a_hbm, targets, rest[-1], brought, chunk)
        for copy in copies:
            copy.start()
        if order is None:
            whole = parts[0]
        else:
            whole = rest.pop(0)
            me = lax.axis_index("row")
            width = parts[0].shape[1]
            for part, m in zip(parts, order):
                whole[:, pl.ds(pl.multiple_of((me ^ m) * width, width), width)] = part[...]
        waited = 0
        for j, out in zip(products, outs):
            if j not in chunks:
                at = brought.index(j)
                for copy in copies[waited : HALVES * (at + 1)]:
                    copy.wait()
                waited = HALVES * (at + 1)
                chunks[j] = targets[at]
            right = chunks[j]

            def one(n, _, right=right, out=out):
                at = pl.ds(pl.multiple_of(n * step, step), step)
                out[:, at] = dot16(whole[...], right[at, :], ((1,), (1,))).astype(out.dtype)
                return _

            lax.fori_loop(0, chunk // step, one, 0)
        for copy in copies[waited:]:
            copy.wait()

    outputs = [shape((block, chunk), f32 if j == 0 else CROSS) for j in products]
    outputs += [shape((chunk, cols), bf16) for _ in brought]
    if order is not None:
        outputs.append(shape((block, cols), bf16))
    return call(
        kernel,
        list(lefts) + list(held.values()) + [matrix],
        outputs,
        "forward_%d" % products[0],
        specs=[VMEM] * (len(lefts) + len(held)) + [ANY],
        scratch=[pltpu.SemaphoreType.DMA((len(brought), HALVES))],
    )


def backward_begin(piece, chunk_j, begun=None):
    given = [] if begun is None else [begun]

    def kernel(p_ref, a_ref, *rest):
        got = dot16(p_ref[...], a_ref[...], ((1,), (0,)))
        rest[-1][...] = rest[0][...] + got if given else got

    name = "backward_more" if given else "backward_own"
    return call(kernel, [piece, chunk_j, *given], [shape((piece.shape[0], chunk_j.shape[1]))], name)[0]


def backward(pieces, chunks, begun, targets, parts):
    groups = len(pieces)
    block = pieces[0].shape[0]
    width = chunks[0].shape[1] // parts

    def kernel(*rest):
        lefts, rights, begun_ref, outs = rest[:groups], rest[groups : 2 * groups], rest[2 * groups], rest[2 * groups + 1 :]
        me = lax.axis_index("row")
        for out, wanted in zip(outs, targets):
            for n, j in enumerate(wanted):
                at = pl.ds(pl.multiple_of((me ^ j) * width, width), width)
                total = begun_ref[:, at]
                for left, right in zip(lefts, rights):
                    total = total + dot16(left[...], right[:, at], ((1,), (0,)))
                out[n] = total

    outputs = [shape((len(wanted), block, width)) for wanted in targets]
    return call(kernel, [*pieces, *chunks, begun], outputs, "backward_%d" % targets[0][0])


def combine(mine, theirs):
    count, block, width = mine.shape

    def kernel(mine_ref, theirs_ref, *outs):
        for n, out in enumerate(outs):
            out[...] = (mine_ref[n] + theirs_ref[n]).astype(CROSS)

    return call(kernel, [mine, theirs], [shape((block, width), CROSS)] * count, "combine")


def coefficients(pieces, turned, total, further=None):
    block, width = pieces[0].shape[-2:]
    size = turned.shape[1] // 2
    half = block // 2
    n_pieces = len(pieces)
    given = [] if further is None else [further]
    count = size + (further.shape[1] if given else 0)

    def kernel(*rest):
        parts, turned_ref = rest[:n_pieces], rest[n_pieces]
        more = rest[n_pieces + 1 : n_pieces + 1 + len(given)]
        image_ref, mine_ref, theirs_ref, held = rest[n_pieces + 1 + len(given) :]
        image = parts[0][...].astype(f32).reshape(block, width)
        for part in parts[1:]:
            image = image + part[...].astype(f32).reshape(block, width)
        image_ref[...] = image
        high, low = split(image)
        right = turned_ref[...]
        got = dot16(high, right, ((1,), (0,)))
        got = got[:, :size] + (got[:, size:] + dot16(low, right[:, :size], ((1,), (0,))))
        held[:, :size] = got * (1.0 / total)
        if more:
            held[:, size:] = more[0][...]
        own = lax.axis_index("row") % 2
        mine_ref[...] = held[pl.ds(pl.multiple_of(own * half, half), half), :]
        theirs_ref[...] = held[pl.ds(pl.multiple_of((1 - own) * half, half), half), :]

    return call(
        kernel,
        [*pieces, turned, *given],
        [shape((block, width)), shape((half, count)), shape((half, count))],
        "coefficients",
        scratch=[pltpu.VMEM((block, count), f32)],
    )


def project(image, rows_high, rows_low, mine, other, total):
    block, width = image.shape
    size = rows_high.shape[0]
    half = block // 2
    count = mine.shape[1]

    def kernel(image_ref, high_ref, low_ref, mine_ref, other_ref, *rest):
        out_ref, round_ref, gram_ref = rest[:3]
        held = rest[-1]
        own = lax.axis_index("row") % 2
        held[pl.ds(pl.multiple_of(own * half, half), half), :] = mine_ref[...]
        held[pl.ds(pl.multiple_of((1 - own) * half, half), half), :] = other_ref[...]
        high, low = split(held[:, :size])
        right = high_ref[...]
        taken = dot16(high, right, ((1,), (0,))) + (
            dot16(low, right, ((1,), (0,))) + dot16(high, low_ref[...], ((1,), (0,)))
        )
        out = image_ref[...] - taken
        high, low = split(out)
        out_ref[...] = out
        round_ref[...] = high
        cross = dot16(high, low, ((1,), (1,))) + dot16(low, high, ((1,), (1,)))
        gram_ref[...] = (dot16(high, high, ((1,), (1,))) + cross) * (1.0 / total)
        if count > size:
            rest[3][...] = held[:, size:]

    outputs = [shape((block, width)), shape((block, width), bf16), shape((block, block))]
    if count > size:
        outputs.append(shape((block, count - size)))
    return call(
        kernel,
        [image, rows_high, rows_low, mine, other],
        outputs,
        "project",
        scratch=[pltpu.VMEM((block, count), f32)],
    )


GROUP = 8


def eliminate(gram):
    block = gram.shape[0]
    line = lax.broadcasted_iota(jnp.int32, (block, block), 0)
    lane = lax.broadcasted_iota(jnp.int32, (block, block), 1)
    both = jnp.concatenate([gram, jnp.where(line == lane, 1.0, 0.0).astype(f32)], 1)
    place = lax.broadcasted_iota(jnp.int32, both.shape, 0)
    for base in range(0, block, GROUP):
        count = min(GROUP, block - base)
        columns = [jnp.broadcast_to(both[:, base + q : base + q + 1], both.shape) for q in range(count)]
        for q in range(count):
            j = base + q
            pivot = 1.0 / columns[q][j : j + 1, :]
            ratio = jnp.where(place > j, columns[q] * pivot, 0.0)
            for p in range(q + 1, count):
                columns[p] = columns[p] - ratio * columns[p][j : j + 1, :]
            both = both - ratio * both[j : j + 1, :]
    upper = both[:, :block]
    diagonal = jnp.sum(jnp.where(line == lane, upper, 0.0), axis=1, keepdims=True)
    scale = 1.0 / jnp.sqrt(diagonal)
    inverse = jnp.where(line >= lane, both[:, block:] * scale, 0.0)
    return jnp.where(lane >= line, upper * scale, 0.0).T, inverse


def factor_left(gram, rows):
    def kernel(gram_ref, rows_ref, low_ref, inverse_ref, new_ref):
        low, inverse = eliminate(gram_ref[...])
        low_ref[...] = low
        inverse_ref[...] = inverse
        new_ref[...] = dot32(inverse, rows_ref[...], ((1,), (0,)))

    small = shape(gram.shape)
    return call(kernel, [gram, rows], [small, small, shape(rows.shape)], "factor_left")


def factor_right(gram, rows, left_low, left_inverse):
    def kernel(gram_ref, rows_ref, left_low_ref, left_inverse_ref, factors_ref, new_ref):
        turn = left_inverse_ref[...]
        gram_here = dot32(dot32(turn, gram_ref[...], ((1,), (0,))), turn, ((1,), (1,)))
        low, inverse = eliminate(gram_here)
        factors_ref[0] = left_low_ref[...]
        factors_ref[1] = low
        new_ref[...] = dot32(dot32(inverse, turn, ((1,), (0,))), rows_ref[...], ((1,), (0,)))

    return call(
        kernel,
        [gram, rows, left_low, left_inverse],
        [shape((2, *gram.shape)), shape(rows.shape)],
        "factor_right",
    )


def bases_split(bases):
    out = []
    for group in bases:
        rows = jnp.concatenate(group, 0)
        rows = jnp.pad(rows, ((0, padded(rows.shape[0]) - rows.shape[0]), (0, 0)))
        high, low = split(rows)
        out += [high, low, jnp.concatenate([high.T, low.T], 1)]
    return out


def shards(matrix, left_basis, right_basis, right_block, *, n_col, n_row):
    total = left_basis.shape[1] * n_col * n_row
    chunk, width = matrix.shape[0] // n_col, matrix.shape[1] // n_row
    tiled = n_col == 4 and n_row == 8 and width % 128 == 0 and chunk % 32 == 0
    row_swap = lambda values, bit: swap(values, "row", n_row, bit)
    col_swap = lambda values, bit: swap(values, "col", n_col, bit)

    def all_sum(values):
        values = values + row_swap(values, 1)
        values = exchange_sum(values, "row", n_row, 2)
        return exchange_sum(values, "col", n_col, 1)

    def split_sum(mine, theirs):
        mine = mine + row_swap(theirs, 1)
        mine = exchange_sum(mine, "row", n_row, 2)
        mine = exchange_sum(mine, "col", n_col, 1)
        return mine, row_swap(mine, 1)

    rounded = right_block.astype(bf16)
    bases = ([left_basis], [right_basis, right_block])
    if tiled:
        lefts = {m: row_swap(rounded, m) for m in range(2, n_row, 2)}
        lefts[0], lefts[1] = rounded, row_swap(rounded, 1)
        chunk_2, *prepared = fetch(matrix, chunk, 2, bases)
        chunk_2, *after = lax.optimization_barrier((chunk_2, *(lefts[m] for m in range(2, n_row, 2))))
        for m, values in zip(range(2, n_row, 2), after):
            lefts[m] = values
            lefts[m + 1] = row_swap(values, 1)
        order = sorted(lefts)
        piece_2, piece_3, chunk_3, chunk_1, whole = forward(
            [lefts[m] for m in order], order, {2: chunk_2}, matrix, chunk, [2, 3], [3, 1]
        )
        piece_1, piece_0, chunk_0 = forward([whole], None, {1: chunk_1}, matrix, chunk, [1, 0], [0])
        pieces = [piece_0, col_swap(piece_1, 1), col_swap(piece_2, 2), col_swap(piece_3, 3)]
    else:
        prepared = bases_split(bases)
        whole = lax.all_gather(rounded, "row", axis=1, tiled=True)
        partial = dot16(whole, matrix, ((1,), (1,)))
        me = lax.axis_index("col")
        pieces = [lax.dynamic_slice_in_dim(partial, (me ^ j) * chunk, chunk, 1) for j in range(n_col)]
        pieces = [pieces[0]] + [col_swap(pieces[j].astype(CROSS), j) for j in range(1, n_col)]
    left_high, left_low, left_turned, right_high, right_low, right_turned = prepared

    image, mine, theirs = coefficients(pieces, left_turned, total)
    mine, other = split_sum(mine, theirs)
    projected, low, gram = project(image, left_high, left_low, mine, other, total)
    lows = [col_swap(low, j) for j in range(1, n_col)]
    if tiled:
        begun = backward_begin(lows[0], chunk_1, backward_begin(low, chunk_0))
        ready = (lows[1:], [chunk_2, chunk_3], begun)
        far = list(range(2, n_row, 2))
        (theirs,) = backward(*ready, [[m + 1 for m in far]], n_row)
        theirs = row_swap(theirs, 1)
        (mine,) = backward(*ready, [far], n_row)
        begun, *sent = lax.optimization_barrier((begun, *combine(mine, theirs)))
        pieces = [row_swap(values, m) for m, values in zip(far, sent)]
        theirs, mine = backward(*ready[:2], begun, [[1], [0]], n_row)
        pieces = [mine, row_swap(theirs, 1)] + pieces
    else:
        me_col, me = lax.axis_index("col"), lax.axis_index("row")
        partial = sum(
            dot16(piece, lax.dynamic_slice_in_dim(matrix, (me_col ^ g) * chunk, chunk, 0), ((1,), (0,)))
            for g, piece in enumerate([low] + lows)
        )
        cut = [lax.dynamic_slice_in_dim(partial, (me ^ j) * width, width, 1) for j in range(n_row)]
        mine = jnp.stack(cut[0::2]) + row_swap(jnp.stack(cut[1::2]), 1)
        pieces = [mine[0]] + [row_swap(mine[m].astype(CROSS), 2 * m) for m in range(1, n_row // 2)]
    coimage, mine, theirs = coefficients(pieces, right_turned, total, gram)
    mine, other = split_sum(mine, theirs)
    coprojected, _, cogram, gram = project(coimage, right_high, right_low, mine, other, total)
    cogram = all_sum(cogram)
    factor, inverse, left_new = factor_left(gram, projected)
    factors, right_new = factor_right(cogram, coprojected, factor, inverse)
    return left_new, right_new, factors


def solution(mesh):
    in_specs = (
        P("row", "col"),
        P(None, ("row", "col")),
        P(None, ("col", "row")),
        P(None, ("col", "row")),
    )
    out_specs = (P(None, ("row", "col")), P(None, ("col", "row")), P())
    body = functools.partial(shards, n_col=mesh.shape["col"], n_row=mesh.shape["row"])
    return jax.shard_map(body, mesh=mesh, in_specs=in_specs, out_specs=out_specs, check_vma=False)
```

```python
import functools

import jax
import jax.numpy as jnp
from jax import lax
from jax.experimental import pallas as pl
from jax.experimental.pallas import tpu as pltpu
from jax.sharding import PartitionSpec as P


f32 = jnp.float32
bf16 = jnp.bfloat16
CROSS = bf16
ANY = pl.BlockSpec(memory_space=pltpu.HBM)
VMEM = pl.BlockSpec(memory_space=pltpu.VMEM)


def dot16(first, second, dims):
    return lax.dot_general(first, second, (dims, ((), ())), preferred_element_type=f32)


def dot32(first, second, dims):
    return lax.dot_general(first, second, (dims, ((), ())), precision=lax.Precision.HIGHEST, preferred_element_type=f32)


def split(values):
    high = values.astype(bf16)
    return high, (values - high.astype(f32)).astype(bf16)


def limit(mebibytes):
    return pltpu.CompilerParams(vmem_limit_bytes=mebibytes << 20)


def shape(dims, dtype=f32):
    return jax.ShapeDtypeStruct(dims, dtype)


def padded(count):
    return -(-count // 128) * 128


def call(kernel, inputs, outputs, specs=None, scratch=(), mebibytes=8):
    return pl.pallas_call(
        kernel,
        in_specs=specs or [VMEM] * len(inputs),
        out_specs=[VMEM] * len(outputs),
        out_shape=outputs,
        scratch_shapes=list(scratch),
        compiler_params=limit(mebibytes),
    )(*inputs)


def swap(values, axis, size, bit):
    return lax.ppermute(values, axis, [(i, i ^ bit) for i in range(size)])


def exchange_sum(values, axis, size, bit):
    while bit < size:
        if bit * 2 < size:
            one, two, three = (swap(values, axis, size, m) for m in (bit, bit * 2, bit * 3))
            values = (values + one) + (two + three)
            bit *= 4
        else:
            values = values + swap(values, axis, size, bit)
            bit *= 2
    return values


HALVES = 2


def fetch_copies(a_hbm, targets, sems, chunks, chunk):
    me = lax.axis_index("col")
    part = chunk // HALVES
    copies = []
    for n, j in enumerate(chunks):
        for h in range(HALVES):
            start = pl.multiple_of((me ^ j) * chunk + h * part, part)
            copies.append(
                pltpu.make_async_copy(
                    a_hbm.at[pl.ds(start, part), :], targets[n].at[pl.ds(h * part, part), :], sems.at[n, h]
                )
            )
    return copies


def fetch(matrix, chunk, j):
    def kernel(a_hbm, target, sems):
        copies = fetch_copies(a_hbm, [target], sems, [j], chunk)
        for copy in copies:
            copy.start()
        for copy in copies:
            copy.wait()

    outputs = [shape((chunk, matrix.shape[1]), bf16)]
    return call(kernel, [matrix], outputs, specs=[ANY], scratch=[pltpu.SemaphoreType.DMA((1, HALVES))], mebibytes=24)[0]


def prepare(bases):
    width = bases[0].shape[1]
    total = sum(b.shape[0] for b in bases)
    size = padded(total)

    def kernel(*rest):
        sources, (rows_high, rows_low, turned) = rest[: len(bases)], rest[len(bases) :]
        if total != size:
            rows_high[...] = jnp.zeros_like(rows_high)
            rows_low[...] = jnp.zeros_like(rows_low)
            turned[...] = jnp.zeros_like(turned)
        at = 0
        for source in sources:
            values = source[...]
            count = values.shape[0]
            high, low = split(values)
            rows_high[at : at + count, :] = high
            rows_low[at : at + count, :] = low
            high, low = split(values.T)
            turned[:, at : at + count] = high
            turned[:, size + at : size + at + count] = low
            at += count

    outputs = [shape((size, width), bf16), shape((size, width), bf16), shape((width, 2 * size), bf16)]
    return call(kernel, list(bases), outputs)


def forward(lefts, order, held, matrix, chunk, products, brought):
    cols = matrix.shape[1]
    block = lefts[0].shape[0]
    step = chunk // 3 if chunk % 384 == 0 else chunk
    source = [matrix] if brought else []

    def kernel(*rest):
        rest = list(rest)
        parts = [rest.pop(0) for _ in lefts]
        chunks = {j: rest.pop(0) for j in held}
        a_hbm = [rest.pop(0) for _ in source]
        outs = [rest.pop(0) for _ in products]
        targets = [rest.pop(0) for _ in brought]
        copies = fetch_copies(a_hbm[0], targets, rest[-1], brought, chunk) if brought else []
        for copy in copies:
            copy.start()
        if order is None:
            whole = parts[0]
        else:
            whole = rest.pop(0)
            me = lax.axis_index("row")
            width = parts[0].shape[1]
            for part, m in zip(parts, order):
                whole[:, pl.ds(pl.multiple_of((me ^ m) * width, width), width)] = part[...]
        waited = 0
        for j, out in zip(products, outs):
            if j not in chunks:
                at = brought.index(j)
                for copy in copies[waited : HALVES * (at + 1)]:
                    copy.wait()
                waited = HALVES * (at + 1)
                chunks[j] = targets[at]
            right = chunks[j]

            def one(n, _, right=right, out=out):
                at = pl.ds(pl.multiple_of(n * step, step), step)
                out[:, at] = dot16(whole[...], right[at, :], ((1,), (1,))).astype(out.dtype)
                return _

            lax.fori_loop(0, chunk // step, one, 0)
        for copy in copies[waited:]:
            copy.wait()

    outputs = [shape((block, chunk), f32 if j == 0 else CROSS) for j in products]
    outputs += [shape((chunk, cols), bf16) for _ in brought]
    if order is not None:
        outputs.append(shape((block, cols), bf16))
    return call(
        kernel,
        list(lefts) + list(held.values()) + source,
        outputs,
        specs=[VMEM] * (len(lefts) + len(held)) + [ANY] * len(source),
        scratch=[pltpu.SemaphoreType.DMA((len(brought), HALVES))] if brought else [],
        mebibytes=8,
    )


def backward_begin(piece, chunk_j, begun=None):
    given = [] if begun is None else [begun]

    def kernel(p_ref, a_ref, *rest):
        got = dot16(p_ref[...], a_ref[...], ((1,), (0,)))
        rest[-1][...] = rest[0][...] + got if given else got

    return call(kernel, [piece, chunk_j, *given], [shape((piece.shape[0], chunk_j.shape[1]))])[0]


def backward(pieces, chunks, begun, targets, parts):
    groups = len(pieces)
    block = pieces[0].shape[0]
    width = chunks[0].shape[1] // parts

    def kernel(*rest):
        lefts, rights, begun_ref, outs = rest[:groups], rest[groups : 2 * groups], rest[2 * groups], rest[2 * groups + 1 :]
        me = lax.axis_index("row")
        for out, wanted in zip(outs, targets):
            for n, j in enumerate(wanted):
                at = pl.ds(pl.multiple_of((me ^ j) * width, width), width)
                total = begun_ref[:, at]
                for left, right in zip(lefts, rights):
                    total = total + dot16(left[...], right[:, at], ((1,), (0,)))
                out[n] = total

    outputs = [shape((len(wanted), block, width)) for wanted in targets]
    return call(kernel, [*pieces, *chunks, begun], outputs)


def combine(mine, theirs):
    count, block, width = mine.shape

    def kernel(mine_ref, theirs_ref, *outs):
        for n, out in enumerate(outs):
            out[...] = (mine_ref[n] + theirs_ref[n]).astype(CROSS)

    return call(kernel, [mine, theirs], [shape((block, width), CROSS)] * count)


def coefficients(pieces, turned, total, further=None):
    block, width = pieces[0].shape[-2:]
    size = turned.shape[1] // 2
    half = block // 2
    n_pieces = len(pieces)
    given = [] if further is None else [further]
    count = size + (further.shape[1] if given else 0)

    def kernel(*rest):
        parts, turned_ref = rest[:n_pieces], rest[n_pieces]
        more = rest[n_pieces + 1 : n_pieces + 1 + len(given)]
        image_ref, mine_ref, theirs_ref, held = rest[n_pieces + 1 + len(given) :]
        image = parts[0][...].astype(f32).reshape(block, width)
        for part in parts[1:]:
            image = image + part[...].astype(f32).reshape(block, width)
        image_ref[...] = image
        high, low = split(image)
        right = turned_ref[...]
        got = dot16(high, right, ((1,), (0,)))
        got = got[:, :size] + (got[:, size:] + dot16(low, right[:, :size], ((1,), (0,))))
        held[:, :size] = got * (1.0 / total)
        if more:
            held[:, size:] = more[0][...]
        own = lax.axis_index("row") % 2
        mine_ref[...] = held[pl.ds(pl.multiple_of(own * half, half), half), :]
        theirs_ref[...] = held[pl.ds(pl.multiple_of((1 - own) * half, half), half), :]

    return call(
        kernel,
        [*pieces, turned, *given],
        [shape((block, width)), shape((half, count)), shape((half, count))],
        scratch=[pltpu.VMEM((block, count), f32)],
    )


def project(image, rows_high, rows_low, mine, other, total):
    block, width = image.shape
    size = rows_high.shape[0]
    half = block // 2
    count = mine.shape[1]

    def kernel(image_ref, high_ref, low_ref, mine_ref, other_ref, *rest):
        out_ref, round_ref, gram_ref = rest[:3]
        held = rest[-1]
        own = lax.axis_index("row") % 2
        held[pl.ds(pl.multiple_of(own * half, half), half), :] = mine_ref[...]
        held[pl.ds(pl.multiple_of((1 - own) * half, half), half), :] = other_ref[...]
        high, low = split(held[:, :size])
        right = high_ref[...]
        taken = dot16(high, right, ((1,), (0,))) + (
            dot16(low, right, ((1,), (0,))) + dot16(high, low_ref[...], ((1,), (0,)))
        )
        out = image_ref[...] - taken
        high, low = split(out)
        out_ref[...] = out
        round_ref[...] = high
        cross = dot16(high, low, ((1,), (1,))) + dot16(low, high, ((1,), (1,)))
        gram_ref[...] = (dot16(high, high, ((1,), (1,))) + cross) * (1.0 / total)
        if count > size:
            rest[3][...] = held[:, size:]

    outputs = [shape((block, width)), shape((block, width), bf16), shape((block, block))]
    if count > size:
        outputs.append(shape((block, count - size)))
    return call(kernel, [image, rows_high, rows_low, mine, other], outputs, scratch=[pltpu.VMEM((block, count), f32)])


GROUP = 8


def eliminate(gram):
    block = gram.shape[0]
    line = lax.broadcasted_iota(jnp.int32, (block, block), 0)
    lane = lax.broadcasted_iota(jnp.int32, (block, block), 1)
    both = jnp.concatenate([gram, jnp.where(line == lane, 1.0, 0.0).astype(f32)], 1)
    place = lax.broadcasted_iota(jnp.int32, both.shape, 0)
    for base in range(0, block, GROUP):
        count = min(GROUP, block - base)
        columns = [jnp.broadcast_to(both[:, base + q : base + q + 1], both.shape) for q in range(count)]
        for q in range(count):
            j = base + q
            pivot = 1.0 / columns[q][j : j + 1, :]
            ratio = jnp.where(place > j, columns[q] * pivot, 0.0)
            for p in range(q + 1, count):
                columns[p] = columns[p] - ratio * columns[p][j : j + 1, :]
            both = both - ratio * both[j : j + 1, :]
    upper = both[:, :block]
    diagonal = jnp.sum(jnp.where(line == lane, upper, 0.0), axis=1, keepdims=True)
    scale = 1.0 / jnp.sqrt(diagonal)
    inverse = jnp.where(line >= lane, both[:, block:] * scale, 0.0)
    return jnp.where(lane >= line, upper * scale, 0.0).T, inverse


def factor_left(gram, rows):
    def kernel(gram_ref, rows_ref, low_ref, inverse_ref, new_ref):
        low, inverse = eliminate(gram_ref[...])
        low_ref[...] = low
        inverse_ref[...] = inverse
        new_ref[...] = dot32(inverse, rows_ref[...], ((1,), (0,)))

    small = shape(gram.shape)
    return call(kernel, [gram, rows], [small, small, shape(rows.shape)])


def factor_right(gram, rows, left_low, left_inverse):
    def kernel(gram_ref, rows_ref, left_low_ref, left_inverse_ref, factors_ref, new_ref):
        turn = left_inverse_ref[...]
        gram_here = dot32(dot32(turn, gram_ref[...], ((1,), (0,))), turn, ((1,), (1,)))
        low, inverse = eliminate(gram_here)
        factors_ref[0] = left_low_ref[...]
        factors_ref[1] = low
        new_ref[...] = dot32(dot32(inverse, turn, ((1,), (0,))), rows_ref[...], ((1,), (0,)))

    return call(kernel, [gram, rows, left_low, left_inverse], [shape((2, *gram.shape)), shape(rows.shape)])


def bases_split(bases):
    rows = jnp.concatenate(bases, 0)
    rows = jnp.pad(rows, ((0, padded(rows.shape[0]) - rows.shape[0]), (0, 0)))
    high, low = split(rows)
    return high, low, jnp.concatenate([high.T, low.T], 1)


def step(matrix, left_basis, right_basis, right_block, *, n_col, n_row):
    total = left_basis.shape[1] * n_col * n_row
    chunk, width = matrix.shape[0] // n_col, matrix.shape[1] // n_row
    tiled = n_col == 4 and n_row == 8 and width % 128 == 0 and chunk % 32 == 0
    row_swap = lambda values, bit: swap(values, "row", n_row, bit)
    col_swap = lambda values, bit: swap(values, "col", n_col, bit)

    def all_sum(values):
        values = values + row_swap(values, 1)
        values = exchange_sum(values, "row", n_row, 2)
        return exchange_sum(values, "col", n_col, 1)

    def split_sum(mine, theirs):
        mine = mine + row_swap(theirs, 1)
        mine = exchange_sum(mine, "row", n_row, 2)
        mine = exchange_sum(mine, "col", n_col, 1)
        return mine, row_swap(mine, 1)

    rounded = right_block.astype(bf16)
    prepared_rows = prepare if tiled else bases_split
    if tiled:
        lefts = {m: row_swap(rounded, m) for m in range(2, n_row, 2)}
        lefts[0], lefts[1] = rounded, row_swap(rounded, 1)
        chunk_2 = fetch(matrix, chunk, 2)
        chunk_2, *after = lax.optimization_barrier((chunk_2, *(lefts[m] for m in range(2, n_row, 2))))
        for m, values in zip(range(2, n_row, 2), after):
            lefts[m] = values
            lefts[m + 1] = row_swap(values, 1)
        order = sorted(lefts)
        piece_2, piece_3, chunk_3, chunk_1, whole = forward(
            [lefts[m] for m in order], order, {2: chunk_2}, matrix, chunk, [2, 3], [3, 1]
        )
        piece_1, chunk_0 = forward([whole], None, {1: chunk_1}, matrix, chunk, [1], [0])
        (piece_0,) = forward([whole], None, {0: chunk_0}, matrix, chunk, [0], [])
        pieces = [piece_0, col_swap(piece_1, 1), col_swap(piece_2, 2), col_swap(piece_3, 3)]
    else:
        whole = lax.all_gather(rounded, "row", axis=1, tiled=True)
        partial = dot16(whole, matrix, ((1,), (1,)))
        me = lax.axis_index("col")
        pieces = [lax.dynamic_slice_in_dim(partial, (me ^ j) * chunk, chunk, 1) for j in range(n_col)]
        pieces = [pieces[0]] + [col_swap(pieces[j].astype(CROSS), j) for j in range(1, n_col)]
    if tiled:
        pieces[0], left_basis = lax.optimization_barrier((pieces[0], left_basis))
    left_high, left_low, left_turned = prepared_rows([left_basis])
    image, mine, theirs = coefficients(pieces, left_turned, total)
    if tiled:
        image, right_basis, right_block = lax.optimization_barrier((image, right_basis, right_block))
    right_high, right_low, right_turned = prepared_rows([right_basis, right_block])
    mine, other = split_sum(mine, theirs)
    projected, low, gram = project(image, left_high, left_low, mine, other, total)
    lows = [col_swap(low, j) for j in range(1, n_col)]
    if tiled:
        begun = backward_begin(lows[0], chunk_1, backward_begin(low, chunk_0))
        ready = (lows[1:], [chunk_2, chunk_3], begun)
        far = list(range(2, n_row, 2))
        (theirs,) = backward(*ready, [[m + 1 for m in far]], n_row)
        theirs = row_swap(theirs, 1)
        (mine,) = backward(*ready, [far], n_row)
        begun, *sent = lax.optimization_barrier((begun, *combine(mine, theirs)))
        pieces = [row_swap(values, m) for m, values in zip(far, sent)]
        theirs, mine = backward(*ready[:2], begun, [[1], [0]], n_row)
        pieces = [mine, row_swap(theirs, 1)] + pieces
    else:
        me_col, me = lax.axis_index("col"), lax.axis_index("row")
        partial = sum(
            dot16(piece, lax.dynamic_slice_in_dim(matrix, (me_col ^ g) * chunk, chunk, 0), ((1,), (0,)))
            for g, piece in enumerate([low] + lows)
        )
        cut = [lax.dynamic_slice_in_dim(partial, (me ^ j) * width, width, 1) for j in range(n_row)]
        mine = jnp.stack(cut[0::2]) + row_swap(jnp.stack(cut[1::2]), 1)
        pieces = [mine[0]] + [row_swap(mine[m].astype(CROSS), 2 * m) for m in range(1, n_row // 2)]
    coimage, mine, theirs = coefficients(pieces, right_turned, total, gram)
    mine, other = split_sum(mine, theirs)
    coprojected, _, cogram, gram = project(coimage, right_high, right_low, mine, other, total)
    cogram = all_sum(cogram)
    factor, inverse, left_new = factor_left(gram, projected)
    factors, right_new = factor_right(cogram, coprojected, factor, inverse)
    return left_new, right_new, factors


def solution(mesh):
    in_specs = (
        P("row", "col"),
        P(None, ("row", "col")),
        P(None, ("col", "row")),
        P(None, ("col", "row")),
    )
    out_specs = (P(None, ("row", "col")), P(None, ("col", "row")), P())
    body = functools.partial(step, n_col=mesh.shape["col"], n_row=mesh.shape["row"])
    return jax.shard_map(body, mesh=mesh, in_specs=in_specs, out_specs=out_specs, check_vma=False)
```

```python
import functools

import jax
import jax.numpy as jnp
from jax import lax
from jax.experimental import pallas as pl
from jax.experimental.pallas import tpu as pltpu
from jax.sharding import PartitionSpec as P


f32 = jnp.float32
bf16 = jnp.bfloat16
CROSS = bf16
ANY = pl.BlockSpec(memory_space=pltpu.HBM)
VMEM = pl.BlockSpec(memory_space=pltpu.VMEM)


def dot16(first, second, dims):
    return lax.dot_general(first, second, (dims, ((), ())), preferred_element_type=f32)


def dot32(first, second, dims):
    return lax.dot_general(first, second, (dims, ((), ())), precision=lax.Precision.HIGHEST, preferred_element_type=f32)


def split(values):
    high = values.astype(bf16)
    return high, (values - high.astype(f32)).astype(bf16)


def limit(mebibytes):
    return pltpu.CompilerParams(vmem_limit_bytes=mebibytes << 20)


def shape(dims, dtype=f32):
    return jax.ShapeDtypeStruct(dims, dtype)


def padded(count):
    return -(-count // 128) * 128


def call(kernel, inputs, outputs, specs=None, scratch=(), mebibytes=8):
    return pl.pallas_call(
        kernel,
        in_specs=specs or [VMEM] * len(inputs),
        out_specs=[VMEM] * len(outputs),
        out_shape=outputs,
        scratch_shapes=list(scratch),
        compiler_params=limit(mebibytes),
    )(*inputs)


def swap(values, axis, size, bit):
    return lax.ppermute(values, axis, [(i, i ^ bit) for i in range(size)])


def exchange_sum(values, axis, size, bit):
    while bit < size:
        if bit * 2 < size:
            one, two, three = (swap(values, axis, size, m) for m in (bit, bit * 2, bit * 3))
            values = (values + one) + (two + three)
            bit *= 4
        else:
            values = values + swap(values, axis, size, bit)
            bit *= 2
    return values


HALVES = 2


def fetch_copies(a_hbm, targets, sems, chunks, chunk):
    me = lax.axis_index("col")
    part = chunk // HALVES
    copies = []
    for n, j in enumerate(chunks):
        for h in range(HALVES):
            start = pl.multiple_of((me ^ j) * chunk + h * part, part)
            copies.append(
                pltpu.make_async_copy(
                    a_hbm.at[pl.ds(start, part), :], targets[n].at[pl.ds(h * part, part), :], sems.at[n, h]
                )
            )
    return copies


def fetch(matrix, chunk, j):
    def kernel(a_hbm, target, sems):
        copies = fetch_copies(a_hbm, [target], sems, [j], chunk)
        for copy in copies:
            copy.start()
        for copy in copies:
            copy.wait()

    outputs = [shape((chunk, matrix.shape[1]), bf16)]
    return call(kernel, [matrix], outputs, specs=[ANY], scratch=[pltpu.SemaphoreType.DMA((1, HALVES))], mebibytes=24)[0]


def prepare(bases):
    width = bases[0].shape[1]
    total = sum(b.shape[0] for b in bases)
    size = padded(total)

    def kernel(*rest):
        sources, (rows_high, rows_low, turned) = rest[: len(bases)], rest[len(bases) :]
        if total != size:
            rows_high[...] = jnp.zeros_like(rows_high)
            rows_low[...] = jnp.zeros_like(rows_low)
            turned[...] = jnp.zeros_like(turned)
        at = 0
        for source in sources:
            values = source[...]
            count = values.shape[0]
            high, low = split(values)
            rows_high[at : at + count, :] = high
            rows_low[at : at + count, :] = low
            high, low = split(values.T)
            turned[:, at : at + count] = high
            turned[:, size + at : size + at + count] = low
            at += count

    outputs = [shape((size, width), bf16), shape((size, width), bf16), shape((width, 2 * size), bf16)]
    return call(kernel, list(bases), outputs)


def forward(lefts, order, held, matrix, chunk, products, brought):
    cols = matrix.shape[1]
    block = lefts[0].shape[0]
    step = chunk // 3 if chunk % 384 == 0 else chunk
    source = [matrix] if brought else []

    def kernel(*rest):
        rest = list(rest)
        parts = [rest.pop(0) for _ in lefts]
        chunks = {j: rest.pop(0) for j in held}
        a_hbm = [rest.pop(0) for _ in source]
        outs = [rest.pop(0) for _ in products]
        targets = [rest.pop(0) for _ in brought]
        copies = fetch_copies(a_hbm[0], targets, rest[-1], brought, chunk) if brought else []
        for copy in copies:
            copy.start()
        if order is None:
            whole = parts[0]
        else:
            whole = rest.pop(0)
            me = lax.axis_index("row")
            width = parts[0].shape[1]
            for part, m in zip(parts, order):
                whole[:, pl.ds(pl.multiple_of((me ^ m) * width, width), width)] = part[...]
        waited = 0
        for j, out in zip(products, outs):
            if j not in chunks:
                at = brought.index(j)
                for copy in copies[waited : HALVES * (at + 1)]:
                    copy.wait()
                waited = HALVES * (at + 1)
                chunks[j] = targets[at]
            right = chunks[j]

            def one(n, _, right=right, out=out):
                at = pl.ds(pl.multiple_of(n * step, step), step)
                out[:, at] = dot16(whole[...], right[at, :], ((1,), (1,))).astype(out.dtype)
                return _

            lax.fori_loop(0, chunk // step, one, 0)
        for copy in copies[waited:]:
            copy.wait()

    outputs = [shape((block, chunk), f32 if j == 0 else CROSS) for j in products]
    outputs += [shape((chunk, cols), bf16) for _ in brought]
    if order is not None:
        outputs.append(shape((block, cols), bf16))
    return call(
        kernel,
        list(lefts) + list(held.values()) + source,
        outputs,
        specs=[VMEM] * (len(lefts) + len(held)) + [ANY] * len(source),
        scratch=[pltpu.SemaphoreType.DMA((len(brought), HALVES))] if brought else [],
        mebibytes=8,
    )


def backward_begin(piece, chunk_j, begun=None):
    given = [] if begun is None else [begun]

    def kernel(p_ref, a_ref, *rest):
        got = dot16(p_ref[...], a_ref[...], ((1,), (0,)))
        rest[-1][...] = rest[0][...] + got if given else got

    return call(kernel, [piece, chunk_j, *given], [shape((piece.shape[0], chunk_j.shape[1]))])[0]


def backward(pieces, chunks, begun, targets, parts):
    groups = len(pieces)
    block = pieces[0].shape[0]
    width = chunks[0].shape[1] // parts

    def kernel(*rest):
        lefts, rights, begun_ref, outs = rest[:groups], rest[groups : 2 * groups], rest[2 * groups], rest[2 * groups + 1 :]
        me = lax.axis_index("row")
        for out, wanted in zip(outs, targets):
            for n, j in enumerate(wanted):
                at = pl.ds(pl.multiple_of((me ^ j) * width, width), width)
                total = begun_ref[:, at]
                for left, right in zip(lefts, rights):
                    total = total + dot16(left[...], right[:, at], ((1,), (0,)))
                out[n] = total

    outputs = [shape((len(wanted), block, width)) for wanted in targets]
    return call(kernel, [*pieces, *chunks, begun], outputs)


def combine(mine, theirs):
    count, block, width = mine.shape

    def kernel(mine_ref, theirs_ref, *outs):
        for n, out in enumerate(outs):
            out[...] = (mine_ref[n] + theirs_ref[n]).astype(CROSS)

    return call(kernel, [mine, theirs], [shape((block, width), CROSS)] * count)


def coefficients(pieces, turned, total, further=None):
    block, width = pieces[0].shape[-2:]
    size = turned.shape[1] // 2
    half = block // 2
    n_pieces = len(pieces)
    given = [] if further is None else [further]
    count = size + (further.shape[1] if given else 0)

    def kernel(*rest):
        parts, turned_ref = rest[:n_pieces], rest[n_pieces]
        more = rest[n_pieces + 1 : n_pieces + 1 + len(given)]
        image_ref, mine_ref, theirs_ref, held = rest[n_pieces + 1 + len(given) :]
        image = parts[0][...].astype(f32).reshape(block, width)
        for part in parts[1:]:
            image = image + part[...].astype(f32).reshape(block, width)
        image_ref[...] = image
        high, low = split(image)
        right = turned_ref[...]
        got = dot16(high, right, ((1,), (0,)))
        got = got[:, :size] + (got[:, size:] + dot16(low, right[:, :size], ((1,), (0,))))
        held[:, :size] = got * (1.0 / total)
        if more:
            held[:, size:] = more[0][...]
        own = lax.axis_index("row") % 2
        mine_ref[...] = held[pl.ds(pl.multiple_of(own * half, half), half), :]
        theirs_ref[...] = held[pl.ds(pl.multiple_of((1 - own) * half, half), half), :]

    return call(
        kernel,
        [*pieces, turned, *given],
        [shape((block, width)), shape((half, count)), shape((half, count))],
        scratch=[pltpu.VMEM((block, count), f32)],
    )


def project(image, rows_high, rows_low, mine, other, total):
    block, width = image.shape
    size = rows_high.shape[0]
    half = block // 2
    count = mine.shape[1]

    def kernel(image_ref, high_ref, low_ref, mine_ref, other_ref, *rest):
        out_ref, round_ref, gram_ref = rest[:3]
        held = rest[-1]
        own = lax.axis_index("row") % 2
        held[pl.ds(pl.multiple_of(own * half, half), half), :] = mine_ref[...]
        held[pl.ds(pl.multiple_of((1 - own) * half, half), half), :] = other_ref[...]
        high, low = split(held[:, :size])
        right = high_ref[...]
        taken = dot16(high, right, ((1,), (0,))) + (
            dot16(low, right, ((1,), (0,))) + dot16(high, low_ref[...], ((1,), (0,)))
        )
        out = image_ref[...] - taken
        high, low = split(out)
        out_ref[...] = out
        round_ref[...] = high
        cross = dot16(high, low, ((1,), (1,))) + dot16(low, high, ((1,), (1,)))
        gram_ref[...] = (dot16(high, high, ((1,), (1,))) + cross) * (1.0 / total)
        if count > size:
            rest[3][...] = held[:, size:]

    outputs = [shape((block, width)), shape((block, width), bf16), shape((block, block))]
    if count > size:
        outputs.append(shape((block, count - size)))
    return call(kernel, [image, rows_high, rows_low, mine, other], outputs, scratch=[pltpu.VMEM((block, count), f32)])


GROUP = 8


def eliminate(gram):
    block = gram.shape[0]
    line = lax.broadcasted_iota(jnp.int32, (block, block), 0)
    lane = lax.broadcasted_iota(jnp.int32, (block, block), 1)
    both = jnp.concatenate([gram, jnp.where(line == lane, 1.0, 0.0).astype(f32)], 1)
    place = lax.broadcasted_iota(jnp.int32, both.shape, 0)
    for base in range(0, block, GROUP):
        count = min(GROUP, block - base)
        columns = [jnp.broadcast_to(both[:, base + q : base + q + 1], both.shape) for q in range(count)]
        for q in range(count):
            j = base + q
            pivot = 1.0 / columns[q][j : j + 1, :]
            ratio = jnp.where(place > j, columns[q] * pivot, 0.0)
            for p in range(q + 1, count):
                columns[p] = columns[p] - ratio * columns[p][j : j + 1, :]
            both = both - ratio * both[j : j + 1, :]
    upper = both[:, :block]
    diagonal = jnp.sum(jnp.where(line == lane, upper, 0.0), axis=1, keepdims=True)
    scale = 1.0 / jnp.sqrt(diagonal)
    inverse = jnp.where(line >= lane, both[:, block:] * scale, 0.0)
    return jnp.where(lane >= line, upper * scale, 0.0).T, inverse


def factor_left(gram, rows):
    def kernel(gram_ref, rows_ref, low_ref, inverse_ref, new_ref):
        low, inverse = eliminate(gram_ref[...])
        low_ref[...] = low
        inverse_ref[...] = inverse
        new_ref[...] = dot32(inverse, rows_ref[...], ((1,), (0,)))

    small = shape(gram.shape)
    return call(kernel, [gram, rows], [small, small, shape(rows.shape)])


def factor_right(gram, rows, left_low, left_inverse):
    def kernel(gram_ref, rows_ref, left_low_ref, left_inverse_ref, factors_ref, new_ref):
        low, inverse = eliminate(gram_ref[...])
        new_ref[...] = dot32(inverse, rows_ref[...], ((1,), (0,)))
        factors_ref[0] = left_low_ref[...]
        line = lax.broadcasted_iota(jnp.int32, low.shape, 0)
        lane = lax.broadcasted_iota(jnp.int32, low.shape, 1)
        factors_ref[1] = jnp.where(line >= lane, dot32(left_inverse_ref[...], low, ((1,), (0,))), 0.0)

    return call(kernel, [gram, rows, left_low, left_inverse], [shape((2, *gram.shape)), shape(rows.shape)])


def bases_split(bases):
    rows = jnp.concatenate(bases, 0)
    rows = jnp.pad(rows, ((0, padded(rows.shape[0]) - rows.shape[0]), (0, 0)))
    high, low = split(rows)
    return high, low, jnp.concatenate([high.T, low.T], 1)


def step(matrix, left_basis, right_basis, right_block, *, n_col, n_row):
    total = left_basis.shape[1] * n_col * n_row
    chunk, width = matrix.shape[0] // n_col, matrix.shape[1] // n_row
    tiled = n_col == 4 and n_row == 8 and width % 128 == 0 and chunk % 32 == 0
    row_swap = lambda values, bit: swap(values, "row", n_row, bit)
    col_swap = lambda values, bit: swap(values, "col", n_col, bit)

    def all_sum(values):
        values = values + row_swap(values, 1)
        values = exchange_sum(values, "row", n_row, 2)
        return exchange_sum(values, "col", n_col, 1)

    def split_sum(mine, theirs):
        mine = mine + row_swap(theirs, 1)
        mine = exchange_sum(mine, "row", n_row, 2)
        mine = exchange_sum(mine, "col", n_col, 1)
        return mine, row_swap(mine, 1)

    rounded = right_block.astype(bf16)
    prepared_rows = prepare if tiled else bases_split
    if tiled:
        lefts = {m: row_swap(rounded, m) for m in range(2, n_row, 2)}
        lefts[0], lefts[1] = rounded, row_swap(rounded, 1)
        chunk_2 = fetch(matrix, chunk, 2)
        chunk_2, *after = lax.optimization_barrier((chunk_2, *(lefts[m] for m in range(2, n_row, 2))))
        for m, values in zip(range(2, n_row, 2), after):
            lefts[m] = values
            lefts[m + 1] = row_swap(values, 1)
        order = sorted(lefts)
        piece_2, piece_3, chunk_3, chunk_1, whole = forward(
            [lefts[m] for m in order], order, {2: chunk_2}, matrix, chunk, [2, 3], [3, 1]
        )
        piece_1, chunk_0 = forward([whole], None, {1: chunk_1}, matrix, chunk, [1], [0])
        (piece_0,) = forward([whole], None, {0: chunk_0}, matrix, chunk, [0], [])
        pieces = [piece_0, col_swap(piece_1, 1), col_swap(piece_2, 2), col_swap(piece_3, 3)]
    else:
        whole = lax.all_gather(rounded, "row", axis=1, tiled=True)
        partial = dot16(whole, matrix, ((1,), (1,)))
        me = lax.axis_index("col")
        pieces = [lax.dynamic_slice_in_dim(partial, (me ^ j) * chunk, chunk, 1) for j in range(n_col)]
        pieces = [pieces[0]] + [col_swap(pieces[j].astype(CROSS), j) for j in range(1, n_col)]
    if tiled:
        pieces[0], left_basis = lax.optimization_barrier((pieces[0], left_basis))
    left_high, left_low, left_turned = prepared_rows([left_basis])
    image, mine, theirs = coefficients(pieces, left_turned, total)
    mine, other = split_sum(mine, theirs)
    projected, low, gram = project(image, left_high, left_low, mine, other, total)
    if tiled:
        lows = [col_swap(low, j) for j in range(1, n_col)]
        begun = backward_begin(lows[0], chunk_1, backward_begin(low, chunk_0))
        begun = backward_begin(lows[1], chunk_2, begun)
        begun, right_basis, right_block = lax.optimization_barrier((begun, right_basis, right_block))
        ready = (lows[2:], [chunk_3], begun)
        far = list(range(2, n_row, 2))
        (theirs,) = backward(*ready, [[m + 1 for m in far]], n_row)
        theirs = row_swap(theirs, 1)
        (mine,) = backward(*ready, [far], n_row)
        begun, *sent = lax.optimization_barrier((begun, *combine(mine, theirs)))
        pieces = [row_swap(values, m) for m, values in zip(far, sent)]
        theirs, mine = backward(*ready[:2], begun, [[1], [0]], n_row)
        pieces = [mine, row_swap(theirs, 1)] + pieces
    else:
        lows = [col_swap(low, j) for j in range(1, n_col)]
        me_col, me = lax.axis_index("col"), lax.axis_index("row")
        partial = sum(
            dot16(piece, lax.dynamic_slice_in_dim(matrix, (me_col ^ g) * chunk, chunk, 0), ((1,), (0,)))
            for g, piece in enumerate([low] + lows)
        )
        cut = [lax.dynamic_slice_in_dim(partial, (me ^ j) * width, width, 1) for j in range(n_row)]
        mine = jnp.stack(cut[0::2]) + row_swap(jnp.stack(cut[1::2]), 1)
        pieces = [mine[0]] + [row_swap(mine[m].astype(CROSS), 2 * m) for m in range(1, n_row // 2)]
    right_high, right_low, right_turned = prepared_rows([right_basis, right_block])
    coimage, mine, theirs = coefficients(pieces, right_turned, total, gram)
    mine, other = split_sum(mine, theirs)
    coprojected, _, cogram, gram = project(coimage, right_high, right_low, mine, other, total)
    cogram = all_sum(cogram)
    factor, inverse, left_new = factor_left(gram, projected)
    factors, right_new = factor_right(cogram, coprojected, factor, inverse)
    return left_new, right_new, factors


def solution(mesh):
    in_specs = (
        P("row", "col"),
        P(None, ("row", "col")),
        P(None, ("col", "row")),
        P(None, ("col", "row")),
    )
    out_specs = (P(None, ("row", "col")), P(None, ("col", "row")), P())
    body = functools.partial(step, n_col=mesh.shape["col"], n_row=mesh.shape["row"])
    return jax.shard_map(body, mesh=mesh, in_specs=in_specs, out_specs=out_specs, check_vma=False)
```

```python
import functools

import jax
import jax.numpy as jnp
from jax import lax
from jax.experimental import pallas as pl
from jax.experimental.pallas import tpu as pltpu
from jax.sharding import PartitionSpec as P


f32 = jnp.float32
bf16 = jnp.bfloat16
CROSS = bf16
TILE = 128
ANY = pl.BlockSpec(memory_space=pltpu.HBM)
VMEM = pl.BlockSpec(memory_space=pltpu.VMEM)


def dot16(first, second, dims):
    return lax.dot_general(first, second, (dims, ((), ())), preferred_element_type=f32)


def dot32(first, second, dims):
    return lax.dot_general(first, second, (dims, ((), ())), precision=lax.Precision.HIGHEST, preferred_element_type=f32)


def split(values):
    high = values.astype(bf16)
    return high, (values - high.astype(f32)).astype(bf16)


def limit(mebibytes):
    return pltpu.CompilerParams(vmem_limit_bytes=mebibytes << 20)


def shape(dims, dtype=f32):
    return jax.ShapeDtypeStruct(dims, dtype)


def padded(count):
    return -(-count // 128) * 128


def call(kernel, inputs, outputs, specs=None, scratch=(), mebibytes=8):
    return pl.pallas_call(
        kernel,
        in_specs=specs or [VMEM] * len(inputs),
        out_specs=[VMEM] * len(outputs),
        out_shape=outputs,
        scratch_shapes=list(scratch),
        compiler_params=limit(mebibytes),
    )(*inputs)


def swap(values, axis, size, bit):
    return lax.ppermute(values, axis, [(i, i ^ bit) for i in range(size)])


def exchange_sum(values, axis, size, bit):
    while bit < size:
        if bit * 2 < size:
            one, two, three = (swap(values, axis, size, m) for m in (bit, bit * 2, bit * 3))
            values = (values + one) + (two + three)
            bit *= 4
        else:
            values = values + swap(values, axis, size, bit)
            bit *= 2
    return values


HALVES = 2


def fetch_copies(a_hbm, targets, sems, chunks, chunk):
    me = lax.axis_index("col")
    part = chunk // HALVES
    copies = []
    for n, j in enumerate(chunks):
        for h in range(HALVES):
            start = pl.multiple_of((me ^ j) * chunk + h * part, part)
            copies.append(
                pltpu.make_async_copy(
                    a_hbm.at[pl.ds(start, part), :], targets[n].at[pl.ds(h * part, part), :], sems.at[n, h]
                )
            )
    return copies


def fetch(matrix, chunk, j):
    def kernel(a_hbm, target, sems):
        copies = fetch_copies(a_hbm, [target], sems, [j], chunk)
        for copy in copies:
            copy.start()
        for copy in copies:
            copy.wait()

    outputs = [shape((chunk, matrix.shape[1]), bf16)]
    return call(kernel, [matrix], outputs, specs=[ANY], scratch=[pltpu.SemaphoreType.DMA((1, HALVES))], mebibytes=24)[0]


def prepare(bases, gram_total=None):
    width = bases[0].shape[1]
    total = sum(b.shape[0] for b in bases)
    size = padded(total)

    def kernel(*rest):
        sources, (rows_high, rows_low, turned) = rest[: len(bases)], rest[len(bases) : len(bases) + 3]
        if total != size:
            rows_high[...] = jnp.zeros_like(rows_high)
            rows_low[...] = jnp.zeros_like(rows_low)
            turned[...] = jnp.zeros_like(turned)
        at = 0
        for source in sources:
            values = source[...]
            count = values.shape[0]
            high, low = split(values)
            rows_high[at : at + count, :] = high
            rows_low[at : at + count, :] = low
            high, low = split(values.T)
            turned[:, at : at + count] = high
            turned[:, size + at : size + at + count] = low
            at += count
        if gram_total is not None:
            mine, theirs, held = rest[len(bases) + 3 :]
            gram = dot16(rows_high[...], turned[...], ((1,), (0,)))
            gram = gram[:, :size] + (gram[:, size:] + dot16(rows_low[...], turned[:, :size], ((1,), (0,))))
            gram = gram * (1.0 / gram_total)
            held[:TILE, :TILE] = gram[:TILE, :TILE]
            held[:TILE, TILE:] = gram[TILE : 2 * TILE, : 2 * TILE]
            held[TILE:, :] = gram[2 * TILE :, :]
            own = lax.axis_index("row") % 2
            mine[...] = held[pl.ds(pl.multiple_of(own * TILE, TILE), TILE), :]
            theirs[...] = held[pl.ds(pl.multiple_of((1 - own) * TILE, TILE), TILE), :]

    outputs = [shape((size, width), bf16), shape((size, width), bf16), shape((width, 2 * size), bf16)]
    scratch = []
    if gram_total is not None:
        outputs += [shape((TILE, size))] * 2
        scratch = [pltpu.VMEM((2 * TILE, size), f32)]
    return call(kernel, list(bases), outputs, scratch=scratch)


def quarter_sums(mine, theirs):
    rows = mine.shape[0] // 4

    def kernel(mine_ref, theirs_ref, *rest):
        outs, held = rest[:4], rest[4]
        held[...] = mine_ref[...] + theirs_ref[...]
        chip = lax.axis_index("row") // 2
        for k, out in enumerate(outs):
            out[...] = held[pl.ds(pl.multiple_of((chip ^ k) * rows, rows), rows), :]

    return call(kernel, [mine, theirs], [shape((rows, mine.shape[1]))] * 4, scratch=[pltpu.VMEM(mine.shape, f32)])


def fold(parts):
    def kernel(a, b, c, d, out):
        out[...] = (a[...] + b[...]) + (c[...] + d[...])

    return call(kernel, list(parts), [shape(parts[0].shape)])[0]


def pair(own_part, other_part):
    rows = own_part.shape[0]

    def kernel(own_ref, other_ref, out_ref):
        own = lax.axis_index("row") % 2
        out_ref[pl.ds(pl.multiple_of(own * rows, rows), rows), :] = own_ref[...]
        out_ref[pl.ds(pl.multiple_of((1 - own) * rows, rows), rows), :] = other_ref[...]

    return call(kernel, [own_part, other_part], [shape((2 * rows, own_part.shape[1]))])[0]


def forward(lefts, order, held, matrix, chunk, products, brought):
    cols = matrix.shape[1]
    block = lefts[0].shape[0]
    step = chunk // 3 if chunk % 384 == 0 else chunk
    source = [matrix] if brought else []

    def kernel(*rest):
        rest = list(rest)
        parts = [rest.pop(0) for _ in lefts]
        chunks = {j: rest.pop(0) for j in held}
        a_hbm = [rest.pop(0) for _ in source]
        outs = [rest.pop(0) for _ in products]
        targets = [rest.pop(0) for _ in brought]
        copies = fetch_copies(a_hbm[0], targets, rest[-1], brought, chunk) if brought else []
        for copy in copies:
            copy.start()
        if order is None:
            whole = parts[0]
        else:
            whole = rest.pop(0)
            me = lax.axis_index("row")
            width = parts[0].shape[1]
            for part, m in zip(parts, order):
                whole[:, pl.ds(pl.multiple_of((me ^ m) * width, width), width)] = part[...]
        waited = 0
        for j, out in zip(products, outs):
            if j not in chunks:
                at = brought.index(j)
                for copy in copies[waited : HALVES * (at + 1)]:
                    copy.wait()
                waited = HALVES * (at + 1)
                chunks[j] = targets[at]
            right = chunks[j]

            def one(n, _, right=right, out=out):
                at = pl.ds(pl.multiple_of(n * step, step), step)
                out[:, at] = dot16(whole[...], right[at, :], ((1,), (1,))).astype(out.dtype)
                return _

            lax.fori_loop(0, chunk // step, one, 0)
        for copy in copies[waited:]:
            copy.wait()

    outputs = [shape((block, chunk), f32 if j == 0 else CROSS) for j in products]
    outputs += [shape((chunk, cols), bf16) for _ in brought]
    if order is not None:
        outputs.append(shape((block, cols), bf16))
    return call(
        kernel,
        list(lefts) + list(held.values()) + source,
        outputs,
        specs=[VMEM] * (len(lefts) + len(held)) + [ANY] * len(source),
        scratch=[pltpu.SemaphoreType.DMA((len(brought), HALVES))] if brought else [],
        mebibytes=8,
    )


def backward_begin(piece, chunk_j, begun=None):
    given = [] if begun is None else [begun]

    def kernel(p_ref, a_ref, *rest):
        got = dot16(p_ref[...], a_ref[...], ((1,), (0,)))
        rest[-1][...] = rest[0][...] + got if given else got

    return call(kernel, [piece, chunk_j, *given], [shape((piece.shape[0], chunk_j.shape[1]))])[0]


def backward(pieces, chunks, begun, targets, parts):
    groups = len(pieces)
    block = pieces[0].shape[0]
    width = chunks[0].shape[1] // parts

    def kernel(*rest):
        lefts, rights, begun_ref, outs = rest[:groups], rest[groups : 2 * groups], rest[2 * groups], rest[2 * groups + 1 :]
        me = lax.axis_index("row")
        for out, wanted in zip(outs, targets):
            for n, j in enumerate(wanted):
                at = pl.ds(pl.multiple_of((me ^ j) * width, width), width)
                total = begun_ref[:, at]
                for left, right in zip(lefts, rights):
                    total = total + dot16(left[...], right[:, at], ((1,), (0,)))
                out[n] = total

    outputs = [shape((len(wanted), block, width)) for wanted in targets]
    return call(kernel, [*pieces, *chunks, begun], outputs)


def combine(mine, theirs):
    count, block, width = mine.shape

    def kernel(mine_ref, theirs_ref, *outs):
        for n, out in enumerate(outs):
            out[...] = (mine_ref[n] + theirs_ref[n]).astype(CROSS)

    return call(kernel, [mine, theirs], [shape((block, width), CROSS)] * count)


def coefficients(pieces, turned, total, further=None, with_gram=False):
    block, width = pieces[0].shape[-2:]
    size = turned.shape[1] // 2
    half = block // 2
    n_pieces = len(pieces)
    given = [] if further is None else [further]
    count = size + (further.shape[1] if given else 0) + (block if with_gram else 0)

    def kernel(*rest):
        parts, turned_ref = rest[:n_pieces], rest[n_pieces]
        more = rest[n_pieces + 1 : n_pieces + 1 + len(given)]
        image_ref, mine_ref, theirs_ref, held = rest[n_pieces + 1 + len(given) :]
        image = parts[0][...].astype(f32).reshape(block, width)
        for part in parts[1:]:
            image = image + part[...].astype(f32).reshape(block, width)
        image_ref[...] = image
        high, low = split(image)
        right = turned_ref[...]
        got = dot16(high, right, ((1,), (0,)))
        got = got[:, :size] + (got[:, size:] + dot16(low, right[:, :size], ((1,), (0,))))
        held[:, :size] = got * (1.0 / total)
        if more:
            held[:, size : size + more[0].shape[1]] = more[0][...]
        if with_gram:
            cross = dot16(high, low, ((1,), (1,))) + dot16(low, high, ((1,), (1,)))
            held[:, count - block :] = (dot16(high, high, ((1,), (1,))) + cross) * (1.0 / total)
        own = lax.axis_index("row") % 2
        mine_ref[...] = held[pl.ds(pl.multiple_of(own * half, half), half), :]
        theirs_ref[...] = held[pl.ds(pl.multiple_of((1 - own) * half, half), half), :]

    return call(
        kernel,
        [*pieces, turned, *given],
        [shape((block, width)), shape((half, count)), shape((half, count))],
        scratch=[pltpu.VMEM((block, count), f32)],
    )


def project(image, rows_high, rows_low, mine, other, total):
    block, width = image.shape
    size = rows_high.shape[0]
    half = block // 2
    count = mine.shape[1]

    def kernel(image_ref, high_ref, low_ref, mine_ref, other_ref, *rest):
        out_ref, round_ref, gram_ref = rest[:3]
        held = rest[-1]
        own = lax.axis_index("row") % 2
        held[pl.ds(pl.multiple_of(own * half, half), half), :] = mine_ref[...]
        held[pl.ds(pl.multiple_of((1 - own) * half, half), half), :] = other_ref[...]
        high, low = split(held[:, :size])
        right = high_ref[...]
        taken = dot16(high, right, ((1,), (0,))) + (
            dot16(low, right, ((1,), (0,))) + dot16(high, low_ref[...], ((1,), (0,)))
        )
        out = image_ref[...] - taken
        high, low = split(out)
        out_ref[...] = out
        round_ref[...] = high
        cross = dot16(high, low, ((1,), (1,))) + dot16(low, high, ((1,), (1,)))
        gram_ref[...] = (dot16(high, high, ((1,), (1,))) + cross) * (1.0 / total)
        if count > size:
            rest[3][...] = held[:, size:]

    outputs = [shape((block, width)), shape((block, width), bf16), shape((block, block))]
    if count > size:
        outputs.append(shape((block, count - size)))
    return call(kernel, [image, rows_high, rows_low, mine, other], outputs, scratch=[pltpu.VMEM((block, count), f32)])


GROUP = 8
JOINT = 8


def eliminate_all(grams, group):
    block = grams[0].shape[0]
    line = lax.broadcasted_iota(jnp.int32, (block, block), 0)
    lane = lax.broadcasted_iota(jnp.int32, (block, block), 1)
    unit = jnp.where(line == lane, 1.0, 0.0).astype(f32)
    all_both = [jnp.concatenate([gram, unit], 1) for gram in grams]
    place = lax.broadcasted_iota(jnp.int32, all_both[0].shape, 0)
    for base in range(0, block, group):
        count = min(group, block - base)
        spread = [
            [jnp.broadcast_to(both[:, base + q : base + q + 1], both.shape) for q in range(count)] for both in all_both
        ]
        for q in range(count):
            j = base + q
            for n, columns in enumerate(spread):
                pivot = 1.0 / columns[q][j : j + 1, :]
                ratio = jnp.where(place > j, columns[q] * pivot, 0.0)
                for p in range(q + 1, count):
                    columns[p] = columns[p] - ratio * columns[p][j : j + 1, :]
                all_both[n] = all_both[n] - ratio * all_both[n][j : j + 1, :]
    found = []
    for both in all_both:
        upper = both[:, :block]
        diagonal = jnp.sum(jnp.where(line == lane, upper, 0.0), axis=1, keepdims=True)
        scale = 1.0 / jnp.sqrt(diagonal)
        inverse = jnp.where(line >= lane, both[:, block:] * scale, 0.0)
        found.append((jnp.where(lane >= line, upper * scale, 0.0).T, inverse))
    return found


def eliminate(gram):
    return eliminate_all([gram], GROUP)[0]


def finish(image, rows_high, rows_low, mine, other, quarters, left_rows):
    block, width = image.shape
    size = rows_high.shape[0]
    half = block // 2
    count = mine.shape[1]
    rows = quarters[0].shape[0] // 2

    def kernel(image_ref, high_ref, low_ref, mine_ref, other_ref, q0, q1, q2, q3, left_ref, *rest):
        left_new_ref, right_new_ref, factors_ref, held, near, far = rest
        own = lax.axis_index("row") % 2
        chip = lax.axis_index("row") // 2
        held[pl.ds(pl.multiple_of(own * half, half), half), :] = mine_ref[...]
        held[pl.ds(pl.multiple_of((1 - own) * half, half), half), :] = other_ref[...]
        for k, quarter in enumerate((q0, q1, q2, q3)):
            at = pl.ds(pl.multiple_of((chip ^ k) * rows, rows), rows)
            near[at, :] = quarter[:rows, :]
            far[at, :] = quarter[rows:, :]
        coefs = held[:, :size]
        first, second, third = (coefs[:, n * TILE : (n + 1) * TILE] for n in range(3))
        by_row = ((1,), (0,))
        last = dot32(third, far[...], by_row)
        middle = dot32(second, near[:, TILE:], by_row)
        start = 0.5 * dot32(first, near[:, :TILE], by_row) + middle[:, :TILE] + last[:, :TILE]
        middle = 0.5 * middle[:, TILE:] + last[:, TILE : 2 * TILE]
        weighted = jnp.concatenate([start - first, middle - second, 0.5 * last[:, 2 * TILE :] - third], 1)
        weighted = dot32(weighted, coefs, ((1,), (1,)))
        left_gram = held[:, size : size + block]
        right_gram = held[:, size + block :] + (weighted + weighted.T)

        high, low = split(coefs)
        right = high_ref[...]
        taken = dot16(high, right, by_row) + (dot16(low, right, by_row) + dot16(high, low_ref[...], by_row))
        projected = image_ref[...] - taken
        (left_low, left_inverse), (right_low, right_inverse) = eliminate_all([left_gram, right_gram], JOINT)
        right_new_ref[...] = dot32(right_inverse, projected, by_row)
        left_new_ref[...] = dot32(left_inverse, left_ref[...], by_row)
        line = lax.broadcasted_iota(jnp.int32, (block, block), 0)
        lane = lax.broadcasted_iota(jnp.int32, (block, block), 1)
        factors_ref[0] = left_low
        factors_ref[1] = jnp.where(line >= lane, dot32(left_inverse, right_low, by_row), 0.0)

    return call(
        kernel,
        [image, rows_high, rows_low, mine, other, *quarters, left_rows],
        [shape(left_rows.shape), shape((block, width)), shape((2, block, block))],
        scratch=[pltpu.VMEM((block, count), f32), pltpu.VMEM((TILE, size), f32), pltpu.VMEM((TILE, size), f32)],
    )


def factor_left(gram, rows):
    def kernel(gram_ref, rows_ref, low_ref, inverse_ref, new_ref):
        low, inverse = eliminate(gram_ref[...])
        low_ref[...] = low
        inverse_ref[...] = inverse
        new_ref[...] = dot32(inverse, rows_ref[...], ((1,), (0,)))

    small = shape(gram.shape)
    return call(kernel, [gram, rows], [small, small, shape(rows.shape)])


def factor_right(gram, rows, left_low, left_inverse):
    def kernel(gram_ref, rows_ref, left_low_ref, left_inverse_ref, factors_ref, new_ref):
        low, inverse = eliminate(gram_ref[...])
        new_ref[...] = dot32(inverse, rows_ref[...], ((1,), (0,)))
        factors_ref[0] = left_low_ref[...]
        line = lax.broadcasted_iota(jnp.int32, low.shape, 0)
        lane = lax.broadcasted_iota(jnp.int32, low.shape, 1)
        factors_ref[1] = jnp.where(line >= lane, dot32(left_inverse_ref[...], low, ((1,), (0,))), 0.0)

    return call(kernel, [gram, rows, left_low, left_inverse], [shape((2, *gram.shape)), shape(rows.shape)])


def bases_split(bases):
    rows = jnp.concatenate(bases, 0)
    rows = jnp.pad(rows, ((0, padded(rows.shape[0]) - rows.shape[0]), (0, 0)))
    high, low = split(rows)
    return high, low, jnp.concatenate([high.T, low.T], 1)


def step(matrix, left_basis, right_basis, right_block, *, n_col, n_row):
    total = left_basis.shape[1] * n_col * n_row
    chunk, width = matrix.shape[0] // n_col, matrix.shape[1] // n_row
    tiled = n_col == 4 and n_row == 8 and width % 128 == 0 and chunk % 32 == 0
    row_swap = lambda values, bit: swap(values, "row", n_row, bit)
    col_swap = lambda values, bit: swap(values, "col", n_col, bit)

    def all_sum(values):
        values = values + row_swap(values, 1)
        values = exchange_sum(values, "row", n_row, 2)
        return exchange_sum(values, "col", n_col, 1)

    def split_sum(mine, theirs):
        mine = mine + row_swap(theirs, 1)
        mine = exchange_sum(mine, "row", n_row, 2)
        mine = exchange_sum(mine, "col", n_col, 1)
        return mine, row_swap(mine, 1)

    rounded = right_block.astype(bf16)
    prepared_rows = prepare if tiled else bases_split
    known = tiled and padded(right_basis.shape[0] + right_block.shape[0]) == 3 * TILE
    if tiled:
        lefts = {m: row_swap(rounded, m) for m in range(2, n_row, 2)}
        lefts[0], lefts[1] = rounded, row_swap(rounded, 1)
        chunk_2 = fetch(matrix, chunk, 2)
        chunk_2, *after = lax.optimization_barrier((chunk_2, *(lefts[m] for m in range(2, n_row, 2))))
        for m, values in zip(range(2, n_row, 2), after):
            lefts[m] = values
            lefts[m + 1] = row_swap(values, 1)
        order = sorted(lefts)
        piece_2, piece_3, chunk_3, chunk_1, whole = forward(
            [lefts[m] for m in order], order, {2: chunk_2}, matrix, chunk, [2, 3], [3, 1]
        )
        piece_1, chunk_0 = forward([whole], None, {1: chunk_1}, matrix, chunk, [1], [0])
        (piece_0,) = forward([whole], None, {0: chunk_0}, matrix, chunk, [0], [])
        pieces = [col_swap(piece_2, 2), col_swap(piece_3, 3)]
        pieces = [piece_0, col_swap(piece_1, 1)] + pieces
    else:
        whole = lax.all_gather(rounded, "row", axis=1, tiled=True)
        partial = dot16(whole, matrix, ((1,), (1,)))
        me = lax.axis_index("col")
        pieces = [lax.dynamic_slice_in_dim(partial, (me ^ j) * chunk, chunk, 1) for j in range(n_col)]
        pieces = [pieces[0]] + [col_swap(pieces[j].astype(CROSS), j) for j in range(1, n_col)]
    if tiled:
        pieces[0], left_basis = lax.optimization_barrier((pieces[0], left_basis))
    left_high, left_low, left_turned = prepared_rows([left_basis])
    image, mine, theirs = coefficients(pieces, left_turned, total)
    if known:
        image, right_basis, right_block = lax.optimization_barrier((image, right_basis, right_block))
        right_high, right_low, right_turned, kept, given = prepare([right_basis, right_block], total)
        given = row_swap(given, 1)
        quarters = quarter_sums(kept, given)
        quarters = [values if k == 0 else row_swap(values, 2 * k) for k, values in enumerate(quarters)]
    mine, other = split_sum(mine, theirs)
    projected, low, gram = project(image, left_high, left_low, mine, other, total)
    if tiled:
        lows = [col_swap(low, j) for j in range(1, n_col)]
        begun = backward_begin(lows[0], chunk_1, backward_begin(low, chunk_0))
        begun = backward_begin(lows[1], chunk_2, begun)
        if not known:
            begun, right_basis, right_block = lax.optimization_barrier((begun, right_basis, right_block))
        ready = (lows[2:], [chunk_3], begun)
        far = list(range(2, n_row, 2))
        (theirs,) = backward(*ready, [[m + 1 for m in far]], n_row)
        theirs = row_swap(theirs, 1)
        (mine,) = backward(*ready, [far], n_row)
        begun, *sent = lax.optimization_barrier((begun, *combine(mine, theirs)))
        pieces = [row_swap(values, m) for m, values in zip(far, sent)]
        theirs, mine = backward(*ready[:2], begun, [[1], [0]], n_row)
        pieces = [mine, row_swap(theirs, 1)] + pieces
        if known:
            gram_part = fold(quarters)
            gram_part = exchange_sum(gram_part, "col", n_col, 1)
            gram_other = row_swap(gram_part, 1)
            gram_part = pair(gram_part, gram_other)
    else:
        lows = [col_swap(low, j) for j in range(1, n_col)]
        me_col, me = lax.axis_index("col"), lax.axis_index("row")
        partial = sum(
            dot16(piece, lax.dynamic_slice_in_dim(matrix, (me_col ^ g) * chunk, chunk, 0), ((1,), (0,)))
            for g, piece in enumerate([low] + lows)
        )
        cut = [lax.dynamic_slice_in_dim(partial, (me ^ j) * width, width, 1) for j in range(n_row)]
        mine = jnp.stack(cut[0::2]) + row_swap(jnp.stack(cut[1::2]), 1)
        pieces = [mine[0]] + [row_swap(mine[m].astype(CROSS), 2 * m) for m in range(1, n_row // 2)]
    if known:
        coimage, mine, theirs = coefficients(pieces, right_turned, total, gram, True)
        mine, other = split_sum(mine, theirs)
        quarters = [gram_part] + [row_swap(gram_part, 2 * k) for k in range(1, 4)]
        return tuple(finish(coimage, right_high, right_low, mine, other, quarters, projected))
    right_high, right_low, right_turned = prepared_rows([right_basis, right_block])
    coimage, mine, theirs = coefficients(pieces, right_turned, total, gram)
    mine, other = split_sum(mine, theirs)
    coprojected, _, cogram, gram = project(coimage, right_high, right_low, mine, other, total)
    cogram = all_sum(cogram)
    factor, inverse, left_new = factor_left(gram, projected)
    factors, right_new = factor_right(cogram, coprojected, factor, inverse)
    return left_new, right_new, factors


def solution(mesh):
    in_specs = (
        P("row", "col"),
        P(None, ("row", "col")),
        P(None, ("col", "row")),
        P(None, ("col", "row")),
    )
    out_specs = (P(None, ("row", "col")), P(None, ("col", "row")), P())
    body = functools.partial(step, n_col=mesh.shape["col"], n_row=mesh.shape["row"])
    return jax.shard_map(body, mesh=mesh, in_specs=in_specs, out_specs=out_specs, check_vma=False)
```

```python
import functools

import jax
import jax.numpy as jnp
from jax import lax
from jax.experimental import pallas as pl
from jax.experimental.pallas import tpu as pltpu
from jax.sharding import PartitionSpec as P


f32 = jnp.float32
bf16 = jnp.bfloat16
CROSS = bf16
TILE = 128
ANY = pl.BlockSpec(memory_space=pltpu.HBM)
VMEM = pl.BlockSpec(memory_space=pltpu.VMEM)


def dot16(first, second, dims):
    return lax.dot_general(first, second, (dims, ((), ())), preferred_element_type=f32)


def dot32(first, second, dims):
    return lax.dot_general(first, second, (dims, ((), ())), precision=lax.Precision.HIGHEST, preferred_element_type=f32)


def split(values):
    high = values.astype(bf16)
    return high, (values - high.astype(f32)).astype(bf16)


def dot_split(first, second, dims):
    (a, b), (c, d) = split(first), split(second)
    return dot16(a, c, dims) + (dot16(a, d, dims) + dot16(b, c, dims))


def limit(mebibytes):
    return pltpu.CompilerParams(vmem_limit_bytes=mebibytes << 20)


def shape(dims, dtype=f32):
    return jax.ShapeDtypeStruct(dims, dtype)


def padded(count):
    return -(-count // 128) * 128


def call(kernel, inputs, outputs, specs=None, scratch=(), mebibytes=8):
    return pl.pallas_call(
        kernel,
        in_specs=specs or [VMEM] * len(inputs),
        out_specs=[VMEM] * len(outputs),
        out_shape=outputs,
        scratch_shapes=list(scratch),
        compiler_params=limit(mebibytes),
    )(*inputs)


def swap(values, axis, size, bit):
    return lax.ppermute(values, axis, [(i, i ^ bit) for i in range(size)])


def exchange_sum(values, axis, size, bit):
    while bit < size:
        if bit * 2 < size:
            one, two, three = (swap(values, axis, size, m) for m in (bit, bit * 2, bit * 3))
            values = (values + one) + (two + three)
            bit *= 4
        else:
            values = values + swap(values, axis, size, bit)
            bit *= 2
    return values


HALVES = 2


def fetch_copies(a_hbm, targets, sems, chunks, chunk):
    me = lax.axis_index("col")
    part = chunk // HALVES
    copies = []
    for n, j in enumerate(chunks):
        for h in range(HALVES):
            start = pl.multiple_of((me ^ j) * chunk + h * part, part)
            copies.append(
                pltpu.make_async_copy(
                    a_hbm.at[pl.ds(start, part), :], targets[n].at[pl.ds(h * part, part), :], sems.at[n, h]
                )
            )
    return copies


def fetch(matrix, chunk, j):
    def kernel(a_hbm, target, sems):
        copies = fetch_copies(a_hbm, [target], sems, [j], chunk)
        for copy in copies:
            copy.start()
        for copy in copies:
            copy.wait()

    outputs = [shape((chunk, matrix.shape[1]), bf16)]
    return call(kernel, [matrix], outputs, specs=[ANY], scratch=[pltpu.SemaphoreType.DMA((1, HALVES))], mebibytes=24)[0]


def prepare(bases, gram_total=None):
    width = bases[0].shape[1]
    total = sum(b.shape[0] for b in bases)
    size = padded(total)

    def kernel(*rest):
        sources, (rows_high, rows_low, turned) = rest[: len(bases)], rest[len(bases) : len(bases) + 3]
        if total != size:
            rows_high[...] = jnp.zeros_like(rows_high)
            rows_low[...] = jnp.zeros_like(rows_low)
            turned[...] = jnp.zeros_like(turned)
        at = 0
        for source in sources:
            values = source[...]
            count = values.shape[0]
            high, low = split(values)
            rows_high[at : at + count, :] = high
            rows_low[at : at + count, :] = low
            high, low = split(values.T)
            turned[:, at : at + count] = high
            turned[:, size + at : size + at + count] = low
            at += count
        if gram_total is not None:
            mine, theirs, held = rest[len(bases) + 3 :]
            gram = dot16(rows_high[...], turned[...], ((1,), (0,)))
            gram = gram[:, :size] + (gram[:, size:] + dot16(rows_low[...], turned[:, :size], ((1,), (0,))))
            gram = gram * (1.0 / gram_total)
            held[:TILE, :TILE] = gram[:TILE, :TILE]
            held[:TILE, TILE:] = gram[TILE : 2 * TILE, : 2 * TILE]
            held[TILE:, :] = gram[2 * TILE :, :]
            own = lax.axis_index("row") % 2
            mine[...] = held[pl.ds(pl.multiple_of(own * TILE, TILE), TILE), :]
            theirs[...] = held[pl.ds(pl.multiple_of((1 - own) * TILE, TILE), TILE), :]

    outputs = [shape((size, width), bf16), shape((size, width), bf16), shape((width, 2 * size), bf16)]
    scratch = []
    if gram_total is not None:
        outputs += [shape((TILE, size))] * 2
        scratch = [pltpu.VMEM((2 * TILE, size), f32)]
    return call(kernel, list(bases), outputs, scratch=scratch)


def quarter_sums(mine, theirs):
    rows = mine.shape[0] // 4

    def kernel(mine_ref, theirs_ref, *rest):
        outs, held = rest[:4], rest[4]
        held[...] = mine_ref[...] + theirs_ref[...]
        chip = lax.axis_index("row") // 2
        for k, out in enumerate(outs):
            out[...] = held[pl.ds(pl.multiple_of((chip ^ k) * rows, rows), rows), :]

    return call(kernel, [mine, theirs], [shape((rows, mine.shape[1]))] * 4, scratch=[pltpu.VMEM(mine.shape, f32)])


def fold(parts):
    def kernel(a, b, c, d, out):
        out[...] = (a[...] + b[...]) + (c[...] + d[...])

    return call(kernel, list(parts), [shape(parts[0].shape)])[0]


def pair(own_part, other_part):
    rows = own_part.shape[0]

    def kernel(own_ref, other_ref, out_ref):
        own = lax.axis_index("row") % 2
        out_ref[pl.ds(pl.multiple_of(own * rows, rows), rows), :] = own_ref[...]
        out_ref[pl.ds(pl.multiple_of((1 - own) * rows, rows), rows), :] = other_ref[...]

    return call(kernel, [own_part, other_part], [shape((2 * rows, own_part.shape[1]))])[0]


def forward(lefts, order, held, matrix, chunk, products, brought):
    cols = matrix.shape[1]
    block = lefts[0].shape[0]
    step = chunk // 3 if chunk % 384 == 0 else chunk
    source = [matrix] if brought else []

    def kernel(*rest):
        rest = list(rest)
        parts = [rest.pop(0) for _ in lefts]
        chunks = {j: rest.pop(0) for j in held}
        a_hbm = [rest.pop(0) for _ in source]
        outs = [rest.pop(0) for _ in products]
        targets = [rest.pop(0) for _ in brought]
        copies = fetch_copies(a_hbm[0], targets, rest[-1], brought, chunk) if brought else []
        for copy in copies:
            copy.start()
        if order is None:
            whole = parts[0]
        else:
            whole = rest.pop(0)
            me = lax.axis_index("row")
            width = parts[0].shape[1]
            for part, m in zip(parts, order):
                whole[:, pl.ds(pl.multiple_of((me ^ m) * width, width), width)] = part[...]
        waited = 0
        for j, out in zip(products, outs):
            if j not in chunks:
                at = brought.index(j)
                for copy in copies[waited : HALVES * (at + 1)]:
                    copy.wait()
                waited = HALVES * (at + 1)
                chunks[j] = targets[at]
            right = chunks[j]

            def one(n, _, right=right, out=out):
                at = pl.ds(pl.multiple_of(n * step, step), step)
                out[:, at] = dot16(whole[...], right[at, :], ((1,), (1,))).astype(out.dtype)
                return _

            lax.fori_loop(0, chunk // step, one, 0)
        for copy in copies[waited:]:
            copy.wait()

    outputs = [shape((block, chunk), f32 if j == 0 else CROSS) for j in products]
    outputs += [shape((chunk, cols), bf16) for _ in brought]
    if order is not None:
        outputs.append(shape((block, cols), bf16))
    return call(
        kernel,
        list(lefts) + list(held.values()) + source,
        outputs,
        specs=[VMEM] * (len(lefts) + len(held)) + [ANY] * len(source),
        scratch=[pltpu.SemaphoreType.DMA((len(brought), HALVES))] if brought else [],
        mebibytes=8,
    )


def backward_begin(piece, chunk_j, begun=None):
    given = [] if begun is None else [begun]

    def kernel(p_ref, a_ref, *rest):
        got = dot16(p_ref[...], a_ref[...], ((1,), (0,)))
        rest[-1][...] = rest[0][...] + got if given else got

    return call(kernel, [piece, chunk_j, *given], [shape((piece.shape[0], chunk_j.shape[1]))])[0]


def backward(pieces, chunks, begun, targets, parts):
    groups = len(pieces)
    block = pieces[0].shape[0]
    width = chunks[0].shape[1] // parts

    def kernel(*rest):
        lefts, rights, begun_ref, outs = rest[:groups], rest[groups : 2 * groups], rest[2 * groups], rest[2 * groups + 1 :]
        me = lax.axis_index("row")
        for out, wanted in zip(outs, targets):
            for n, j in enumerate(wanted):
                at = pl.ds(pl.multiple_of((me ^ j) * width, width), width)
                total = begun_ref[:, at]
                for left, right in zip(lefts, rights):
                    total = total + dot16(left[...], right[:, at], ((1,), (0,)))
                out[n] = total

    outputs = [shape((len(wanted), block, width)) for wanted in targets]
    return call(kernel, [*pieces, *chunks, begun], outputs)


def combine(mine, theirs):
    count, block, width = mine.shape

    def kernel(mine_ref, theirs_ref, *outs):
        for n, out in enumerate(outs):
            out[...] = (mine_ref[n] + theirs_ref[n]).astype(CROSS)

    return call(kernel, [mine, theirs], [shape((block, width), CROSS)] * count)


def coefficients(pieces, turned, total, further=None, with_gram=False):
    block, width = pieces[0].shape[-2:]
    size = turned.shape[1] // 2
    half = block // 2
    n_pieces = len(pieces)
    given = [] if further is None else [further]
    count = size + (further.shape[1] if given else 0) + (block if with_gram else 0)

    def kernel(*rest):
        parts, turned_ref = rest[:n_pieces], rest[n_pieces]
        more = rest[n_pieces + 1 : n_pieces + 1 + len(given)]
        image_ref, mine_ref, theirs_ref, held = rest[n_pieces + 1 + len(given) :]
        image = parts[0][...].astype(f32).reshape(block, width)
        for part in parts[1:]:
            image = image + part[...].astype(f32).reshape(block, width)
        image_ref[...] = image
        high, low = split(image)
        right = turned_ref[...]
        got = dot16(high, right, ((1,), (0,)))
        got = got[:, :size] + (got[:, size:] + dot16(low, right[:, :size], ((1,), (0,))))
        held[:, :size] = got * (1.0 / total)
        if more:
            held[:, size : size + more[0].shape[1]] = more[0][...]
        if with_gram:
            cross = dot16(high, low, ((1,), (1,))) + dot16(low, high, ((1,), (1,)))
            held[:, count - block :] = (dot16(high, high, ((1,), (1,))) + cross) * (1.0 / total)
        own = lax.axis_index("row") % 2
        mine_ref[...] = held[pl.ds(pl.multiple_of(own * half, half), half), :]
        theirs_ref[...] = held[pl.ds(pl.multiple_of((1 - own) * half, half), half), :]

    return call(
        kernel,
        [*pieces, turned, *given],
        [shape((block, width)), shape((half, count)), shape((half, count))],
        scratch=[pltpu.VMEM((block, count), f32)],
    )


def project(image, rows_high, rows_low, mine, other, total):
    block, width = image.shape
    size = rows_high.shape[0]
    half = block // 2
    count = mine.shape[1]

    def kernel(image_ref, high_ref, low_ref, mine_ref, other_ref, *rest):
        out_ref, round_ref, gram_ref = rest[:3]
        held = rest[-1]
        own = lax.axis_index("row") % 2
        held[pl.ds(pl.multiple_of(own * half, half), half), :] = mine_ref[...]
        held[pl.ds(pl.multiple_of((1 - own) * half, half), half), :] = other_ref[...]
        high, low = split(held[:, :size])
        right = high_ref[...]
        taken = dot16(high, right, ((1,), (0,))) + (
            dot16(low, right, ((1,), (0,))) + dot16(high, low_ref[...], ((1,), (0,)))
        )
        out = image_ref[...] - taken
        high, low = split(out)
        out_ref[...] = out
        round_ref[...] = high
        cross = dot16(high, low, ((1,), (1,))) + dot16(low, high, ((1,), (1,)))
        gram_ref[...] = (dot16(high, high, ((1,), (1,))) + cross) * (1.0 / total)
        if count > size:
            rest[3][...] = held[:, size:]

    outputs = [shape((block, width)), shape((block, width), bf16), shape((block, block))]
    if count > size:
        outputs.append(shape((block, count - size)))
    return call(kernel, [image, rows_high, rows_low, mine, other], outputs, scratch=[pltpu.VMEM((block, count), f32)])


GROUP = 8
JOINT = 8


def eliminate_all(grams, group):
    block = grams[0].shape[0]
    line = lax.broadcasted_iota(jnp.int32, (block, block), 0)
    lane = lax.broadcasted_iota(jnp.int32, (block, block), 1)
    unit = jnp.where(line == lane, 1.0, 0.0).astype(f32)
    all_both = [jnp.concatenate([gram, unit], 1) for gram in grams]
    place = lax.broadcasted_iota(jnp.int32, all_both[0].shape, 0)
    for base in range(0, block, group):
        count = min(group, block - base)
        spread = [
            [jnp.broadcast_to(both[:, base + q : base + q + 1], both.shape) for q in range(count)] for both in all_both
        ]
        for q in range(count):
            j = base + q
            for n, columns in enumerate(spread):
                pivot = 1.0 / columns[q][j : j + 1, :]
                ratio = jnp.where(place > j, columns[q] * pivot, 0.0)
                for p in range(q + 1, count):
                    columns[p] = columns[p] - ratio * columns[p][j : j + 1, :]
                all_both[n] = all_both[n] - ratio * all_both[n][j : j + 1, :]
    found = []
    for both in all_both:
        upper = both[:, :block]
        diagonal = jnp.sum(jnp.where(line == lane, upper, 0.0), axis=1, keepdims=True)
        scale = 1.0 / jnp.sqrt(diagonal)
        inverse = jnp.where(line >= lane, both[:, block:] * scale, 0.0)
        found.append((jnp.where(lane >= line, upper * scale, 0.0).T, inverse))
    return found


def eliminate(gram):
    return eliminate_all([gram], GROUP)[0]


def finish(image, rows_high, rows_low, mine, other, quarters, left_rows):
    block, width = image.shape
    size = rows_high.shape[0]
    half = block // 2
    count = mine.shape[1]
    rows = quarters[0].shape[0] // 2

    def kernel(image_ref, high_ref, low_ref, mine_ref, other_ref, q0, q1, q2, q3, left_ref, *rest):
        left_new_ref, right_new_ref, factors_ref, held, near, far = rest
        own = lax.axis_index("row") % 2
        chip = lax.axis_index("row") // 2
        held[pl.ds(pl.multiple_of(own * half, half), half), :] = mine_ref[...]
        held[pl.ds(pl.multiple_of((1 - own) * half, half), half), :] = other_ref[...]
        for k, quarter in enumerate((q0, q1, q2, q3)):
            at = pl.ds(pl.multiple_of((chip ^ k) * rows, rows), rows)
            near[at, :] = quarter[:rows, :]
            far[at, :] = quarter[rows:, :]
        coefs = held[:, :size]
        first, second, third = (coefs[:, n * TILE : (n + 1) * TILE] for n in range(3))
        by_row = ((1,), (0,))
        last = dot_split(third, far[...], by_row)
        middle = dot_split(second, near[:, TILE:], by_row)
        start = 0.5 * dot_split(first, near[:, :TILE], by_row) + middle[:, :TILE] + last[:, :TILE]
        middle = 0.5 * middle[:, TILE:] + last[:, TILE : 2 * TILE]
        weighted = jnp.concatenate([start - first, middle - second, 0.5 * last[:, 2 * TILE :] - third], 1)
        weighted = dot_split(weighted, coefs, ((1,), (1,)))
        left_gram = held[:, size : size + block]
        right_gram = held[:, size + block :] + (weighted + weighted.T)

        high, low = split(coefs)
        right = high_ref[...]
        taken = dot16(high, right, by_row) + (dot16(low, right, by_row) + dot16(high, low_ref[...], by_row))
        projected = image_ref[...] - taken
        (left_low, left_inverse), (right_low, right_inverse) = eliminate_all([left_gram, right_gram], JOINT)
        right_new_ref[...] = dot32(right_inverse, projected, by_row)
        left_new_ref[...] = dot32(left_inverse, left_ref[...], by_row)
        line = lax.broadcasted_iota(jnp.int32, (block, block), 0)
        lane = lax.broadcasted_iota(jnp.int32, (block, block), 1)
        factors_ref[0] = left_low
        factors_ref[1] = jnp.where(line >= lane, dot32(left_inverse, right_low, by_row), 0.0)

    return call(
        kernel,
        [image, rows_high, rows_low, mine, other, *quarters, left_rows],
        [shape(left_rows.shape), shape((block, width)), shape((2, block, block))],
        scratch=[pltpu.VMEM((block, count), f32), pltpu.VMEM((TILE, size), f32), pltpu.VMEM((TILE, size), f32)],
    )


def factor_left(gram, rows):
    def kernel(gram_ref, rows_ref, low_ref, inverse_ref, new_ref):
        low, inverse = eliminate(gram_ref[...])
        low_ref[...] = low
        inverse_ref[...] = inverse
        new_ref[...] = dot32(inverse, rows_ref[...], ((1,), (0,)))

    small = shape(gram.shape)
    return call(kernel, [gram, rows], [small, small, shape(rows.shape)])


def factor_right(gram, rows, left_low, left_inverse):
    def kernel(gram_ref, rows_ref, left_low_ref, left_inverse_ref, factors_ref, new_ref):
        low, inverse = eliminate(gram_ref[...])
        new_ref[...] = dot32(inverse, rows_ref[...], ((1,), (0,)))
        factors_ref[0] = left_low_ref[...]
        line = lax.broadcasted_iota(jnp.int32, low.shape, 0)
        lane = lax.broadcasted_iota(jnp.int32, low.shape, 1)
        factors_ref[1] = jnp.where(line >= lane, dot32(left_inverse_ref[...], low, ((1,), (0,))), 0.0)

    return call(kernel, [gram, rows, left_low, left_inverse], [shape((2, *gram.shape)), shape(rows.shape)])


def bases_split(bases):
    rows = jnp.concatenate(bases, 0)
    rows = jnp.pad(rows, ((0, padded(rows.shape[0]) - rows.shape[0]), (0, 0)))
    high, low = split(rows)
    return high, low, jnp.concatenate([high.T, low.T], 1)


def step(matrix, left_basis, right_basis, right_block, *, n_col, n_row):
    total = left_basis.shape[1] * n_col * n_row
    chunk, width = matrix.shape[0] // n_col, matrix.shape[1] // n_row
    tiled = n_col == 4 and n_row == 8 and width % 128 == 0 and chunk % 32 == 0
    row_swap = lambda values, bit: swap(values, "row", n_row, bit)
    col_swap = lambda values, bit: swap(values, "col", n_col, bit)

    def all_sum(values):
        values = values + row_swap(values, 1)
        values = exchange_sum(values, "row", n_row, 2)
        return exchange_sum(values, "col", n_col, 1)

    def split_sum(mine, theirs):
        mine = mine + row_swap(theirs, 1)
        mine = exchange_sum(mine, "row", n_row, 2)
        mine = exchange_sum(mine, "col", n_col, 1)
        return mine, row_swap(mine, 1)

    rounded = right_block.astype(bf16)
    prepared_rows = prepare if tiled else bases_split
    known = tiled and padded(right_basis.shape[0] + right_block.shape[0]) == 3 * TILE
    if tiled:
        lefts = {m: row_swap(rounded, m) for m in range(2, n_row, 2)}
        lefts[0], lefts[1] = rounded, row_swap(rounded, 1)
        chunk_2 = fetch(matrix, chunk, 2)
        chunk_2, *after = lax.optimization_barrier((chunk_2, *(lefts[m] for m in range(2, n_row, 2))))
        for m, values in zip(range(2, n_row, 2), after):
            lefts[m] = values
            lefts[m + 1] = row_swap(values, 1)
        order = sorted(lefts)
        piece_2, piece_3, chunk_3, chunk_1, whole = forward(
            [lefts[m] for m in order], order, {2: chunk_2}, matrix, chunk, [2, 3], [3, 1]
        )
        piece_1, chunk_0 = forward([whole], None, {1: chunk_1}, matrix, chunk, [1], [0])
        (piece_0,) = forward([whole], None, {0: chunk_0}, matrix, chunk, [0], [])
        pieces = [col_swap(piece_2, 2), col_swap(piece_3, 3)]
        pieces = [piece_0, col_swap(piece_1, 1)] + pieces
    else:
        whole = lax.all_gather(rounded, "row", axis=1, tiled=True)
        partial = dot16(whole, matrix, ((1,), (1,)))
        me = lax.axis_index("col")
        pieces = [lax.dynamic_slice_in_dim(partial, (me ^ j) * chunk, chunk, 1) for j in range(n_col)]
        pieces = [pieces[0]] + [col_swap(pieces[j].astype(CROSS), j) for j in range(1, n_col)]
    if tiled:
        pieces[0], left_basis = lax.optimization_barrier((pieces[0], left_basis))
    left_high, left_low, left_turned = prepared_rows([left_basis])
    image, mine, theirs = coefficients(pieces, left_turned, total)
    if known:
        image, right_basis, right_block = lax.optimization_barrier((image, right_basis, right_block))
        right_high, right_low, right_turned, kept, given = prepare([right_basis, right_block], total)
        given = row_swap(given, 1)
        quarters = quarter_sums(kept, given)
        quarters = [values if k == 0 else row_swap(values, 2 * k) for k, values in enumerate(quarters)]
    mine, other = split_sum(mine, theirs)
    projected, low, gram = project(image, left_high, left_low, mine, other, total)
    if tiled:
        lows = [col_swap(low, j) for j in range(1, n_col)]
        begun = backward_begin(lows[0], chunk_1, backward_begin(low, chunk_0))
        begun = backward_begin(lows[1], chunk_2, begun)
        if not known:
            begun, right_basis, right_block = lax.optimization_barrier((begun, right_basis, right_block))
        ready = (lows[2:], [chunk_3], begun)
        far = list(range(2, n_row, 2))
        (theirs,) = backward(*ready, [[m + 1 for m in far]], n_row)
        theirs = row_swap(theirs, 1)
        (mine,) = backward(*ready, [far], n_row)
        begun, *sent = lax.optimization_barrier((begun, *combine(mine, theirs)))
        pieces = [row_swap(values, m) for m, values in zip(far, sent)]
        theirs, mine = backward(*ready[:2], begun, [[1], [0]], n_row)
        pieces = [mine, row_swap(theirs, 1)] + pieces
        if known:
            gram_part = fold(quarters)
            gram_part = exchange_sum(gram_part, "col", n_col, 1)
            gram_other = row_swap(gram_part, 1)
            gram_part = pair(gram_part, gram_other)
    else:
        lows = [col_swap(low, j) for j in range(1, n_col)]
        me_col, me = lax.axis_index("col"), lax.axis_index("row")
        partial = sum(
            dot16(piece, lax.dynamic_slice_in_dim(matrix, (me_col ^ g) * chunk, chunk, 0), ((1,), (0,)))
            for g, piece in enumerate([low] + lows)
        )
        cut = [lax.dynamic_slice_in_dim(partial, (me ^ j) * width, width, 1) for j in range(n_row)]
        mine = jnp.stack(cut[0::2]) + row_swap(jnp.stack(cut[1::2]), 1)
        pieces = [mine[0]] + [row_swap(mine[m].astype(CROSS), 2 * m) for m in range(1, n_row // 2)]
    if known:
        coimage, mine, theirs = coefficients(pieces, right_turned, total, gram, True)
        mine, other = split_sum(mine, theirs)
        quarters = [gram_part] + [row_swap(gram_part, 2 * k) for k in range(1, 4)]
        return tuple(finish(coimage, right_high, right_low, mine, other, quarters, projected))
    right_high, right_low, right_turned = prepared_rows([right_basis, right_block])
    coimage, mine, theirs = coefficients(pieces, right_turned, total, gram)
    mine, other = split_sum(mine, theirs)
    coprojected, _, cogram, gram = project(coimage, right_high, right_low, mine, other, total)
    cogram = all_sum(cogram)
    factor, inverse, left_new = factor_left(gram, projected)
    factors, right_new = factor_right(cogram, coprojected, factor, inverse)
    return left_new, right_new, factors


def solution(mesh):
    in_specs = (
        P("row", "col"),
        P(None, ("row", "col")),
        P(None, ("col", "row")),
        P(None, ("col", "row")),
    )
    out_specs = (P(None, ("row", "col")), P(None, ("col", "row")), P())
    body = functools.partial(step, n_col=mesh.shape["col"], n_row=mesh.shape["row"])
    return jax.shard_map(body, mesh=mesh, in_specs=in_specs, out_specs=out_specs, check_vma=False)
```
